128 devices in a mesh: row: 16 (over z_hi, y, core), col: 8 (over x, z_lo).
Axes of the slice: x: 4, y: 4, z: 4 (z_hi: 2, z_lo: 2; z = z_hi * 2 + z_lo), core: 2. Of those that a mesh axis runs over, the one named last changes fastest.
Arguments:
- amplitudes: float32 [16384, 16384], P('row', 'col'), may hold values from -2 to 2
- factors: bfloat16 [16384, 768], P(('row', 'col')), may hold values from -0.0234375 to 0.0234375
- energies: float32 [16384], replicated, may hold values from 0.5 to 2
Outputs:
- amplitude_out: float32 [16384, 16384], P('row', 'col')
The draws below stay inside these ranges and needn't reach their ends.
All inputs are finite; a program needn't handle non-finite values.
Results may differ from the reference program's by a relative error of at most 0.0074.
Values may be sent and summed in bfloat16 or wider, within the bound.
A program may use at most 128 MiB of HBM per device.

```python
import math
import jax
import jax.numpy as jnp

ORDER = 16384
AUX = 768
ITERS = 2


def draw_amplitudes(key, part):
    raw = jax.random.normal(key, (ORDER, ORDER), jnp.float32)
    symmetric = (raw + raw.T) * 0.3
    return jnp.clip(symmetric, -2.0, 2.0)


def shard_levels(key, dims, pieces, least, top_value):
    level = 1.0
    for axis_at, parts in pieces:
        draws = jax.random.uniform(jax.random.fold_in(jax.random.fold_in(key, 6), axis_at), (parts,), jnp.float32, least / len(pieces), top_value / len(pieces))
        level = level * jnp.repeat(jnp.exp(draws), dims[axis_at] // parts).reshape((-1,) + (1,) * (len(dims) - 1 - axis_at))
    return level


def normal_values(own_key, shape, deviation, most, cuts=(), dtype=jnp.bfloat16):
    array = jax.random.normal(own_key, shape, jnp.float32) * deviation
    if len(cuts) > 0:
        array = shard_levels(own_key, shape, cuts, -0.22, 0.18) * array
    return jnp.clip(array, min=-most, max=most).astype(dtype)


def setup_inputs(seed: int = 0) -> dict:
    splits = jax.random.split(jax.random.key(seed), 4)
    amplitudes = draw_amplitudes(jax.random.fold_in(splits[3], 71), 0)
    factors = normal_values(splits[1], (ORDER, AUX), (4 * ORDER) ** -0.5, 0.0234375, ((0, 128),))
    energies = jnp.clip(jnp.exp(jax.random.uniform(splits[2], (ORDER,), jnp.float32, math.log(0.5), math.log(2.0))), 0.5, 2.0)
    return dict(amplitudes=amplitudes, factors=factors, energies=energies)


def reference(amplitudes, factors, energies):
    coupling = ORDER / math.sqrt(AUX)
    inv_root = 1.0 / math.sqrt(ORDER)
    denominator = energies[:, None] + energies[None, :]
    amplitude = amplitudes
    for sweep in range(ITERS):
        rounded = amplitude.astype(jnp.bfloat16)
        summed = jnp.dot(rounded, factors, preferred_element_type=jnp.float32) * inv_root
        dressed = (factors.astype(jnp.float32) + summed).astype(jnp.bfloat16)
        residual = jnp.dot(dressed, dressed.T, preferred_element_type=jnp.float32)
        amplitude = -coupling * residual / denominator
    return amplitude
```

```python
import functools
import math

import jax
import jax.numpy as jnp
from jax import lax
from jax.experimental import pallas as pl
from jax.experimental.pallas import tpu as pltpu
from jax.sharding import PartitionSpec as P

ORDER = 16384
AUX = 768
COUPLING = ORDER / math.sqrt(AUX)
INV_ROOT = 1.0 / math.sqrt(ORDER)
MESH = pl.DeviceIdType.MESH
BF16, F32 = jnp.bfloat16, jnp.float32

SLOT = 128
HALF = SLOT // 2
NT = (((1,), (1,)), ((), ()))
TN = (((0,), (0,)), ((), ()))


def rows_at(ref, slot, offset=0, size=SLOT):
    return ref.at[pl.ds(pl.multiple_of(slot * SLOT + offset, HALF), size), :]


class Line:
    def __init__(self, p, m, z, core, own, own_z, sp, sp_z, sm, sm_z, so, so_z):
        self.p, self.m, self.z, self.core = p, m, z, core
        self.own, self.own_z = own, own_z
        self.sp, self.sp_z = sp, sp_z
        self.sm, self.sm_z = sm, sm_z
        self.so, self.so_z = so, so_z


class Gather:
    def __init__(self, line, buf, send, recv, base=0, other=None):
        self.line, self.buf, self.send, self.recv = line, buf, send, recv
        self.base, self.other = base, other
        self.started = []

    def copy(self, i, src, dst, target):
        return pltpu.make_async_remote_copy(
            src_ref=src, dst_ref=dst, send_sem=self.send.at[i], recv_sem=self.recv.at[i],
            device_id=target, device_id_type=MESH,
        )

    def push(self, i, slot, target, offset=0, size=SLOT, src=None):
        dst = rows_at(self.buf, self.base + slot, offset, size)
        c = self.copy(i, dst if src is None else src, dst, target)
        c.start()
        self.started.append(c)

    def arrived(self, i, slot, source, offset=0, size=SLOT):
        dst = rows_at(self.buf, self.base + slot, offset, size)
        self.copy(i, dst, dst, source).wait_recv()

    def to_core(self, i, slot):
        if self.other is not None:
            self.push(9 + i, slot, self.line.core)

    def start(self, src=None):
        ln = self.line
        self.push(0, ln.own, ln.p, src=src)
        self.push(1, ln.own, ln.m, src=src)
        self.push(2, ln.own, ln.z, src=src)
        self.to_core(0, ln.own)

    def pair(self):
        ln = self.line
        self.arrived(2, ln.own_z, ln.z)
        self.push(3, ln.own_z, ln.p)
        self.push(4, ln.own_z, ln.m)
        self.to_core(1, ln.own_z)

    def forward(self):
        ln = self.line
        self.arrived(0, ln.sm, ln.m)
        self.push(5, ln.sm, ln.p, 0, HALF)
        self.to_core(2, ln.sm)
        self.arrived(1, ln.sp, ln.p)
        self.push(6, ln.sp, ln.m, HALF, HALF)
        self.to_core(3, ln.sp)

    def forward_pair(self):
        ln = self.line
        self.arrived(3, ln.sm_z, ln.m)
        self.push(7, ln.sm_z, ln.p, 0, HALF)
        self.to_core(4, ln.sm_z)
        self.arrived(4, ln.sp_z, ln.p)
        self.push(8, ln.sp_z, ln.m, HALF, HALF)
        self.to_core(5, ln.sp_z)

    def last(self):
        ln = self.line
        self.arrived(5, ln.so, ln.m, 0, HALF)
        self.arrived(6, ln.so, ln.p, HALF, HALF)
        self.to_core(6, ln.so)
        self.arrived(7, ln.so_z, ln.m, 0, HALF)
        self.arrived(8, ln.so_z, ln.p, HALF, HALF)
        self.to_core(7, ln.so_z)

    def finish(self):
        ln = self.line
        if self.other is not None:
            order = (ln.own, ln.own_z, ln.sm, ln.sp, ln.sm_z, ln.sp_z, ln.so, ln.so_z)
            for i, slot in enumerate(order):
                dst = rows_at(self.buf, self.other + slot)
                self.copy(9 + i, dst, dst, ln.core).wait_recv()
        for c in self.started:
            c.wait_send()
        self.started = []


class Reduce:
    def __init__(self, line, part, out1, out2, outz, in1, in2, inz, send, recv):
        self.line, self.part = line, part
        self.out1, self.out2, self.outz = out1, out2, outz
        self.in1, self.in2, self.inz = in1, in2, inz
        self.send, self.recv = send, recv
        self.started = []

    def copy(self, i, src, dst, target):
        return pltpu.make_async_remote_copy(
            src_ref=src, dst_ref=dst, send_sem=self.send.at[i], recv_sem=self.recv.at[i],
            device_id=target, device_id_type=MESH,
        )

    def go(self, i, src, dst, target):
        c = self.copy(i, src, dst, target)
        c.start()
        self.started.append(c)

    def get(self, slot, offset, size=HALF):
        return rows_at(self.part, slot, offset, size)[...]

    def opposite(self):
        ln = self.line
        for d, (off, target) in enumerate(((0, ln.p), (HALF, ln.m))):
            self.out1[d, 0:HALF, :] = self.get(ln.so, off).astype(BF16)
            self.out1[d, HALF:SLOT, :] = self.get(ln.so_z, off).astype(BF16)
            self.go(d, self.out1.at[d], self.in1.at[d], target)

    def direct(self, d):
        ln = self.line
        slots, off, target = ((ln.sp, ln.sp_z), HALF, ln.p) if d == 0 else ((ln.sm, ln.sm_z), 0, ln.m)
        self.out2[d, 0, 0:HALF, :] = self.get(slots[0], off).astype(BF16)
        self.out2[d, 0, HALF:SLOT, :] = self.get(slots[1], off).astype(BF16)
        self.go(2 + d, self.out2.at[d, 0], self.in2.at[d, 0], target)

    def dependent(self):
        ln = self.line
        for d in range(2):
            slots, off, target, source = (
                ((ln.sp, ln.sp_z), 0, ln.p, ln.m) if d == 0 else ((ln.sm, ln.sm_z), HALF, ln.m, ln.p)
            )
            self.copy(d, self.in1.at[d], self.in1.at[d], source).wait_recv()
            for h in range(2):
                rows = slice(h * HALF, (h + 1) * HALF)
                total = self.get(slots[h], off) + self.in1[d, rows, :].astype(F32)
                self.out2[d, 1, rows, :] = total.astype(BF16)
            self.go(4 + d, self.out2.at[d, 1], self.in2.at[d, 1], target)

    def summed(self, slot, which):
        rows = slice(which * HALF, (which + 1) * HALF)
        first = self.get(slot, 0) + self.in2[0, 1, rows, :].astype(F32) + self.in2[1, 0, rows, :].astype(F32)
        second = self.get(slot, HALF) + self.in2[0, 0, rows, :].astype(F32) + self.in2[1, 1, rows, :].astype(F32)
        return first, second

    def pair(self):
        ln = self.line
        for d, source in ((0, ln.m), (1, ln.p)):
            self.copy(2 + d, self.in2.at[d, 0], self.in2.at[d, 0], source).wait_recv()
            self.copy(4 + d, self.in2.at[d, 1], self.in2.at[d, 1], source).wait_recv()
        first, second = self.summed(ln.own_z, 1)
        self.outz[0:HALF, :] = first.astype(BF16)
        self.outz[HALF:SLOT, :] = second.astype(BF16)
        self.go(6, self.outz, self.inz, ln.z)

    def dress(self, factors, out):
        ln = self.line
        self.copy(6, self.inz, self.inz, ln.z).wait_recv()
        first, second = self.summed(ln.own, 0)
        for off, total in ((0, first), (HALF, second)):
            rows = pl.ds(off, HALF)
            total = total + self.inz[rows, :].astype(F32)
            out.at[rows, :][...] = (factors.at[rows, :][...].astype(F32) + total).astype(BF16)

    def finish(self):
        for c in self.started:
            c.wait_send()
        self.started = []


def cycle(
    amp, own, energy, dr1, dc1,
    a, stage, fr, fc, dr0, dc0, part_r, part_c, core_out, core_in,
    x1o, x2o, xzo, x1i, x2i, xzi,
    y1o, y2o, yzo, y1i, y2i, yzi,
    e_row, e_col,
    amp_sem, t_sem, agx_s, agx_r, agy_s, agy_r, rsx_s, rsx_r, rsy_s, rsy_r, co_s, co_r,
):
    row, col = lax.axis_index("row"), lax.axis_index("col")
    core, chip_row = lax.rem(row, 2), row // 2
    hi, y = chip_row // 4, lax.rem(chip_row, 4)
    x, lo = col // 2, lax.rem(col, 2)

    def at(r, c):
        return {"row": r, "col": c}

    def x_slot(step, flip):
        return lax.rem(x + step, 4) * 2 + (1 - lo if flip else lo)

    def y_slot(step, flip):
        return (1 - hi if flip else hi) * 4 + lax.rem(y + step, 4)

    def dev_x(step, flip):
        return at(row, x_slot(step, flip))

    def dev_y(step, flip):
        return at(y_slot(step, flip) * 2 + core, col)

    partner = at(chip_row * 2 + 1 - core, col)
    line_x = Line(
        dev_x(1, False), dev_x(3, False), dev_x(0, True), None,
        x_slot(0, False), x_slot(0, True), x_slot(1, False), x_slot(1, True),
        x_slot(3, False), x_slot(3, True), x_slot(2, False), x_slot(2, True),
    )
    line_y = Line(
        dev_y(1, False), dev_y(3, False), dev_y(0, True), partner,
        y_slot(0, False), y_slot(0, True), y_slot(1, False), y_slot(1, True),
        y_slot(3, False), y_slot(3, True), y_slot(2, False), y_slot(2, True),
    )
    mirror = at(col * 2 + core, chip_row)
    off_diagonal = chip_row != col

    def amp_copy(i):
        return pltpu.make_async_copy(amp.at[pl.ds(i * 256, 256), :], stage.at[i % 2], amp_sem.at[i % 2])

    amp_copy(0).start()
    amp_copy(1).start()

    barrier = pltpu.get_barrier_semaphore()
    for ln in (line_x, line_y):
        for device in (ln.p, ln.m, ln.z):
            pl.semaphore_signal(barrier, inc=1, device_id=device, device_id_type=MESH)
    pl.semaphore_signal(barrier, inc=1, device_id=partner, device_id_type=MESH)

    @pl.when(off_diagonal)
    def _():
        pl.semaphore_signal(barrier, inc=1, device_id=mirror, device_id_type=MESH)

    for j in range(8):
        v = energy[pl.ds(row * 8 + j, 1), :]
        e_row[j * 128 : (j + 1) * 128, :] = jnp.broadcast_to(v, (128, 128)).T
    for j in range(16):
        e_col[:, j * 128 : (j + 1) * 128] = energy[pl.ds(col * 16 + j, 1), :]

    @pl.when(off_diagonal)
    def _():
        pl.semaphore_wait(barrier, 8)

    @pl.when(jnp.logical_not(off_diagonal))
    def _():
        pl.semaphore_wait(barrier, 7)

    half_c, other_c = core * 8, (1 - core) * 8
    gx = Gather(line_x, fr, agx_s.at[0], agx_r.at[0])
    gy = Gather(line_y, fc, agy_s.at[0], agy_r.at[0], half_c, other_c)
    gx.start(src=own)
    mine_c = rows_at(fc, half_c + chip_row)
    theirs = rows_at(fc, half_c + col)
    t_send = pltpu.make_async_remote_copy(
        src_ref=own, dst_ref=theirs, send_sem=t_sem.at[0], recv_sem=t_sem.at[1],
        device_id=mirror, device_id_type=MESH,
    )

    @pl.when(off_diagonal)
    def _():
        t_send.start()

    rows_at(fr, line_x.own)[...] = own[...]

    @pl.when(jnp.logical_not(off_diagonal))
    def _():
        mine_c[...] = own[...]

    for i in range(4):
        amp_copy(i).wait()
        a[i * 256 : (i + 1) * 256, :] = stage[i % 2].astype(BF16)
        if i + 2 < 4:
            amp_copy(i + 2).start()

    gx.pair()
    gx.forward()
    gx.forward_pair()

    @pl.when(off_diagonal)
    def _():
        pltpu.make_async_remote_copy(
            src_ref=own, dst_ref=mine_c, send_sem=t_sem.at[0], recv_sem=t_sem.at[1],
            device_id=mirror, device_id_type=MESH,
        ).wait_recv()

    gy.start()
    gx.last()

    def mm_rows(s):
        at_rows = pl.ds(pl.multiple_of((s // 2) * 256, 256), 256)
        part_r[at_rows, :] = (
            jnp.dot(a[at_rows, :], fc[...], preferred_element_type=F32) * INV_ROOT
        )

    def mm_cols(half, s, s_z):
        lhs = [
            a[:, pl.ds(pl.multiple_of((half + i) * SLOT, SLOT), SLOT)] for i in (s, s_z)
        ]
        lhs = jnp.concatenate(lhs, axis=1)
        return lax.dot_general(lhs, fr[...], TN, preferred_element_type=F32) * INV_ROOT

    pairs_y = (
        (line_y.so, line_y.so_z), (line_y.sp, line_y.sp_z), (line_y.sm, line_y.sm_z), (line_y.own, line_y.own_z),
    )

    for it in range(2):
        rsx = Reduce(
            line_x, part_r, x1o, x2o, xzo, x1i.at[it], x2i.at[it], xzi.at[it], rsx_s.at[it], rsx_r.at[it]
        )
        rsy = Reduce(
            line_y, part_c, y1o, y2o, yzo, y1i.at[it], y2i.at[it], yzi.at[it], rsy_s.at[it], rsy_r.at[it]
        )

        def core_copy(i):
            return pltpu.make_async_remote_copy(
                src_ref=core_out.at[i], dst_ref=core_in.at[it, i],
                send_sem=co_s.at[it, i], recv_sem=co_r.at[it, i],
                device_id=partner, device_id_type=MESH,
            )

        def other_half(i):
            core_out[i] = mm_cols(other_c, *pairs_y[i]).astype(BF16)
            core_copy(i).start()

        def own_half(i):
            value = mm_cols(half_c, *pairs_y[i])
            core_copy(i).wait_recv()
            value = value + core_in[it, i].astype(F32)
            rows_at(part_c, pairs_y[i][0])[...] = value[:SLOT]
            rows_at(part_c, pairs_y[i][1])[...] = value[SLOT:]

        if it == 0:
            other_half(0)
            other_half(1)
            gy.forward()
            gy.pair()
            other_half(2)
            other_half(3)
            own_half(0)
            own_half(1)
            gy.forward_pair()
            own_half(2)
            own_half(3)
            gy.last()
            rsy.opposite()
            rsy.direct(0)
            rsy.direct(1)
            gy.finish()
            mm_rows(line_x.so)
            rsx.opposite()
            mm_rows(line_x.sp)
            rsx.direct(0)
            mm_rows(line_x.sm)
            rsx.direct(1)
            rsy.dependent()
            mm_rows(line_x.own)
            rsx.dependent()
        else:
            for i in range(4):
                other_half(i)
            mm_rows(line_x.so)
            rsx.opposite()
            own_half(0)
            rsy.opposite()
            mm_rows(line_x.sp)
            rsx.direct(0)
            mm_rows(line_x.sm)
            rsx.direct(1)
            own_half(1)
            rsy.direct(0)
            own_half(2)
            rsy.direct(1)
            rsx.dependent()
            mm_rows(line_x.own)
            rsy.dependent()
            own_half(3)
        rsy.pair()
        rsx.pair()

        dr, dc = (dr0, dc0) if it == 0 else (dr1, dc1)
        hx = Gather(line_x, dr, agx_s.at[it + 1], agx_r.at[it + 1])
        hy = Gather(line_y, dc, agy_s.at[it + 1], agy_r.at[it + 1], half_c, other_c)
        rsy.dress(mine_c, rows_at(dc, half_c + chip_row))
        hy.start()
        rsx.dress(own, rows_at(dr, line_x.own))
        hx.start()
        hx.pair()
        hy.forward()
        hx.forward()
        hy.pair()
        hx.forward_pair()
        hy.forward_pair()
        hx.last()
        hy.last()
        for i in range(4):
            core_copy(i).wait_send()
        rsx.finish()
        rsy.finish()
        hx.finish()
        hy.finish()

        if it == 0:

            @pl.loop(0, 4)
            def _(i):
                at_rows = pl.ds(pl.multiple_of(i * 256, 256), 256)
                for j in range(4):
                    cols = slice(j * 512, (j + 1) * 512)
                    residual = lax.dot_general(
                        dr0[at_rows, :], dc0[cols, :], NT, preferred_element_type=F32
                    )
                    den = jnp.concatenate([e_row[at_rows, :]] * 4, axis=1) + e_col[:, cols]
                    a[at_rows, cols] = (-COUPLING * residual / den).astype(BF16)

    gx.finish()

    @pl.when(off_diagonal)
    def _():
        t_send.wait_send()


def dma(*shape):
    return pltpu.SemaphoreType.DMA(shape)


def shards(amplitudes, factors, energies):
    row_tile, col_tile = amplitudes.shape
    vmem = pl.BlockSpec(memory_space=pltpu.VMEM)

    def line_buffers():
        return [
            pltpu.VMEM((2, SLOT, AUX), BF16),
            pltpu.VMEM((2, 2, SLOT, AUX), BF16),
            pltpu.VMEM((SLOT, AUX), BF16),
            pltpu.VMEM((2, 2, SLOT, AUX), BF16),
            pltpu.VMEM((2, 2, 2, SLOT, AUX), BF16),
            pltpu.VMEM((2, SLOT, AUX), BF16),
        ]

    dr, dc = pl.pallas_call(
        cycle,
        out_shape=(
            jax.ShapeDtypeStruct((row_tile, AUX), BF16),
            jax.ShapeDtypeStruct((col_tile, AUX), BF16),
        ),
        in_specs=[pl.BlockSpec(memory_space=pl.ANY), vmem, vmem],
        out_specs=(vmem, vmem),
        scratch_shapes=[
            pltpu.VMEM((row_tile, col_tile), BF16),
            pltpu.VMEM((2, 256, col_tile), F32),
            pltpu.VMEM((row_tile, AUX), BF16),
            pltpu.VMEM((col_tile, AUX), BF16),
            pltpu.VMEM((row_tile, AUX), BF16),
            pltpu.VMEM((col_tile, AUX), BF16),
            pltpu.VMEM((row_tile, AUX), F32),
            pltpu.VMEM((row_tile, AUX), F32),
            pltpu.VMEM((4, 256, AUX), BF16),
            pltpu.VMEM((2, 4, 256, AUX), BF16),
            *line_buffers(),
            *line_buffers(),
            pltpu.VMEM((row_tile, 128), F32),
            pltpu.VMEM((1, col_tile), F32),
            dma(2), dma(2),
            dma(3, 9), dma(3, 9), dma(3, 17), dma(3, 17),
            dma(2, 7), dma(2, 7), dma(2, 7), dma(2, 7),
            dma(2, 4), dma(2, 4),
        ],
        compiler_params=pltpu.CompilerParams(
            collective_id=0, has_side_effects=True, vmem_limit_bytes=60 * 1024 * 1024
        ),
        name="cycle",
    )(amplitudes, factors, energies.reshape(128, 128))

    row_energy = lax.dynamic_slice_in_dim(energies, lax.axis_index("row") * row_tile, row_tile)
    col_energy = lax.dynamic_slice_in_dim(energies, lax.axis_index("col") * col_tile, col_tile)
    residual = lax.dot_general(dr, dc, NT, preferred_element_type=F32)
    return -COUPLING * residual / (row_energy[:, None] + col_energy[None, :])


def solution(mesh):
    placed = (P("row", "col"), P(("row", "col"), None), P())
    return jax.shard_map(
        shards, mesh=mesh, in_specs=placed, out_specs=P("row", "col"), check_vma=False
    )
```

```python
import functools
import math

import jax
import jax.numpy as jnp
from jax import lax
from jax.experimental import pallas as pl
from jax.experimental.pallas import tpu as pltpu
from jax.sharding import PartitionSpec as P

ORDER = 16384
AUX = 768
COUPLING = ORDER / math.sqrt(AUX)
INV_ROOT = 1.0 / math.sqrt(ORDER)
MESH = pl.DeviceIdType.MESH
BF16, F32 = jnp.bfloat16, jnp.float32

SLOT = 128
HALF = SLOT // 2
K = AUX // 2
NT = (((1,), (1,)), ((), ()))
TN = (((0,), (0,)), ((), ()))


def part_of(ref, slot, k=None, offset=0, size=SLOT):
    rows = pl.ds(pl.multiple_of(slot * SLOT + offset, HALF), size)
    return ref.at[rows, :] if k is None else ref.at[rows, pl.ds(k * K, K)]


class Line:
    def __init__(self, device, slot, core=None):
        self.p, self.m, self.o, self.z = device(1, 0), device(3, 0), device(2, 0), device(0, 1)
        self.core = core
        self.own, self.own_z = slot(0, 0), slot(0, 1)
        self.sp, self.sp_z = slot(1, 0), slot(1, 1)
        self.sm, self.sm_z = slot(3, 0), slot(3, 1)
        self.so, self.so_z = slot(2, 0), slot(2, 1)


class Exchange:
    def __init__(self, send, recv):
        self.send, self.recv = send, recv
        self.started = []

    def copy(self, i, src, dst, target):
        return pltpu.make_async_remote_copy(
            src_ref=src, dst_ref=dst, send_sem=self.send.at[i], recv_sem=self.recv.at[i],
            device_id=target, device_id_type=MESH,
        )

    def go(self, i, src, dst, target):
        c = self.copy(i, src, dst, target)
        c.start()
        self.started.append(c)

    def got(self, i, dst, source):
        self.copy(i, dst, dst, source).wait_recv()

    def sent(self):
        for c in self.started:
            c.wait_send()
        self.started = []


class Gather(Exchange):
    def __init__(self, line, buf, k, send, recv, base=0, other=None, relay_own=False, relay_pair=False):
        super().__init__(send, recv)
        self.line, self.buf, self.k = line, buf, k
        self.base, self.other = base, other
        self.relay_own, self.relay_pair = relay_own, relay_pair

    def view(self, slot, offset=0, size=SLOT):
        return part_of(self.buf, self.base + slot, self.k, offset, size)

    def push(self, i, slot, target, offset=0, size=SLOT, src=None):
        dst = self.view(slot, offset, size)
        self.go(i, dst if src is None else src, dst, target)

    def arrived(self, i, slot, source, offset=0, size=SLOT):
        self.got(i, self.view(slot, offset, size), source)

    def to_core(self, i, slot):
        if self.other is not None:
            self.push(9 + i, slot, self.line.core)

    def start(self, src=None):
        ln = self.line
        self.push(2, ln.own, ln.z, src=src)
        if not self.relay_own:
            self.push(5, ln.own, ln.o, src=src)
        self.push(0, ln.own, ln.p, src=src)
        self.push(1, ln.own, ln.m, src=src)
        self.to_core(0, ln.own)

    def pair(self):
        ln = self.line
        self.arrived(2, ln.own_z, ln.z)
        if not self.relay_pair:
            self.push(7, ln.own_z, ln.o)
        self.push(3, ln.own_z, ln.p)
        self.push(4, ln.own_z, ln.m)
        self.to_core(1, ln.own_z)

    def near(self):
        ln = self.line
        self.arrived(0, ln.sm, ln.m)
        if self.relay_own:
            self.push(5, ln.sm, ln.p, 0, HALF)
        self.to_core(2, ln.sm)
        self.arrived(1, ln.sp, ln.p)
        if self.relay_own:
            self.push(6, ln.sp, ln.m, HALF, HALF)
        self.to_core(3, ln.sp)

    def near_pair(self):
        ln = self.line
        self.arrived(3, ln.sm_z, ln.m)
        if self.relay_pair:
            self.push(7, ln.sm_z, ln.p, 0, HALF)
        self.to_core(4, ln.sm_z)
        self.arrived(4, ln.sp_z, ln.p)
        if self.relay_pair:
            self.push(8, ln.sp_z, ln.m, HALF, HALF)
        self.to_core(5, ln.sp_z)

    def far(self):
        ln = self.line
        if self.relay_own:
            self.arrived(5, ln.so, ln.m, 0, HALF)
            self.arrived(6, ln.so, ln.p, HALF, HALF)
        else:
            self.arrived(5, ln.so, ln.o)
        self.to_core(6, ln.so)

    def far_pair(self):
        ln = self.line
        if self.relay_pair:
            self.arrived(7, ln.so_z, ln.m, 0, HALF)
            self.arrived(8, ln.so_z, ln.p, HALF, HALF)
        else:
            self.arrived(7, ln.so_z, ln.o)
        self.to_core(7, ln.so_z)

    def from_core(self):
        ln = self.line
        order = (ln.own, ln.own_z, ln.sm, ln.sp, ln.sm_z, ln.sp_z, ln.so, ln.so_z)
        for i, slot in enumerate(order):
            self.got(9 + i, part_of(self.buf, self.other + slot, self.k), ln.core)


class Reduce(Exchange):
    def __init__(self, line, part, out, outz, into, inz, send, recv):
        super().__init__(send, recv)
        self.line, self.part = line, part
        self.out, self.outz, self.into, self.inz = out, outz, into, inz

    def give(self, d):
        ln = self.line
        slots, target = (
            ((ln.sp_z, ln.sp), ln.p), ((ln.sm_z, ln.sm), ln.m), ((ln.so_z, ln.so), ln.o),
        )[d]
        for h in range(2):
            self.out[d, h] = part_of(self.part, slots[h])[...].astype(BF16)
            self.go(2 * d + h, self.out.at[d, h], self.into.at[d, h], target)

    def collect(self, h):
        ln = self.line
        for d, source in ((0, ln.m), (1, ln.p), (2, ln.o)):
            self.got(2 * d + h, self.into.at[d, h], source)
        total = part_of(self.part, ln.own if h else ln.own_z)[...]
        for d in range(3):
            total = total + self.into[d, h].astype(F32)
        return total

    def pair(self):
        self.outz[...] = self.collect(0).astype(BF16)
        self.go(6, self.outz, self.inz, self.line.z)

    def total(self):
        total = self.collect(1)
        self.got(6, self.inz, self.line.z)
        return total + self.inz[...].astype(F32)


def cycle(
    amp, own, energy, dr1, dc1,
    a, stage, fr, fc, own_c, dr0, dc0, part_r, part_c, core_out, core_in,
    x_out, x_outz, x_in, x_inz, y_out, y_outz, y_in, y_inz,
    e_row, e_col,
    amp_sem, turn_s, turn_r, agx_s, agx_r, agy_s, agy_r, rsx_s, rsx_r, rsy_s, rsy_r, co_s, co_r,
):
    row, col = lax.axis_index("row"), lax.axis_index("col")
    core, chip_row = lax.rem(row, 2), row // 2
    hi, y = chip_row // 4, lax.rem(chip_row, 4)
    x, lo = col // 2, lax.rem(col, 2)

    def at(r, c):
        return {"row": r, "col": c}

    def x_slot(step, flip):
        return lax.rem(x + step, 4) * 2 + (1 - lo if flip else lo)

    first_y = lax.rem(x, 2) * 2 + lo
    parity = x // 2 + lo

    def y_slot(step, flip):
        z = 1 - hi if flip else hi
        return lax.rem(x + y + step + 4 - first_y, 4) * 2 + lax.rem(z + parity, 2)

    def dev_x(step, flip):
        return at(row, x_slot(step, flip))

    def dev_y(step, flip):
        z = 1 - hi if flip else hi
        return at((z * 4 + lax.rem(y + step, 4)) * 2 + core, col)

    partner = at(chip_row * 2 + 1 - core, col)
    line_x = Line(dev_x, x_slot)
    line_y = Line(dev_y, y_slot, partner)

    x_to = chip_row // 2
    y_to = lax.rem(y + x + 4 - x_to, 4)
    hi_to = lax.rem(hi + lo + y, 2)
    to_row, to_col = (hi_to * 4 + y_to) * 2 + core, x_to * 2 + lax.rem(y, 2)
    turn_to = at(to_row, to_col)
    turn_from = at(col * 2 + core, line_y.own)
    moves = (to_row - row) * (to_row - row) + (to_col - col) * (to_col - col) != 0
    stays = jnp.logical_not(moves)

    half_c, other_c = core * 8, (1 - core) * 8
    mine_r, mine_c = line_x.own, half_c + line_y.own

    def turn(i, src, dst, device):
        return pltpu.make_async_remote_copy(
            src_ref=src, dst_ref=dst, send_sem=turn_s.at[i], recv_sem=turn_r.at[i],
            device_id=device, device_id_type=MESH,
        )

    def amp_copy(i):
        return pltpu.make_async_copy(amp.at[pl.ds(i * 256, 256), :], stage.at[i % 2], amp_sem.at[i % 2])

    amp_copy(0).start()
    amp_copy(1).start()

    barrier = pltpu.get_barrier_semaphore()

    def greet(device):
        pl.semaphore_signal(barrier, inc=1, device_id=device, device_id_type=MESH)

    for ln in (line_x, line_y):
        for device in (ln.p, ln.m, ln.o, ln.z):
            greet(device)
    greet(partner)

    @pl.when(moves)
    def _():
        greet(turn_to)
        greet(turn_from)

    for j in range(8):
        v = energy[pl.ds(row * 8 + j, 1), :]
        e_row[j * 128 : (j + 1) * 128, :] = jnp.broadcast_to(v, (128, 128)).T
    for j in range(16):
        e_col[:, j * 128 : (j + 1) * 128] = energy[pl.ds(col * 16 + j, 1), :]

    @pl.when(moves)
    def _():
        pl.semaphore_wait(barrier, 11)

    @pl.when(stays)
    def _():
        pl.semaphore_wait(barrier, 9)

    gx = Gather(line_x, fr, None, agx_s.at[0], agx_r.at[0])
    gy = Gather(line_y, fc, None, agy_s.at[0], agy_r.at[0], half_c, other_c)
    own0, own1 = own.at[:, pl.ds(0, K)], own.at[:, pl.ds(K, K)]
    turn_f0 = turn(0, own0, part_of(fc, half_c + col), turn_to)
    turn_f1 = turn(1, own1, own_c, turn_to)

    @pl.when(moves)
    def _():
        turn_f0.start()

    gx.start(src=own1)

    @pl.when(moves)
    def _():
        turn_f1.start()

    part_of(fr, mine_r)[...] = own1[...]

    @pl.when(stays)
    def _():
        part_of(fc, mine_c)[...] = own0[...]
        own_c[...] = own1[...]

    for i in range(4):
        amp_copy(i).wait()
        a[i * 256 : (i + 1) * 256, :] = stage[i % 2].astype(BF16)
        if i + 2 < 4:
            amp_copy(i + 2).start()

    gx.pair()

    @pl.when(moves)
    def _():
        turn(0, own0, part_of(fc, mine_c), turn_from).wait_recv()

    gy.start()
    gx.near()
    gx.far()
    gy.pair()
    gx.near_pair()
    gx.far_pair()

    def mm_rows(s):
        at_rows = pl.ds(pl.multiple_of((s // 2) * 256, 256), 256)
        part_r[at_rows, :] = jnp.dot(a[at_rows, :], fc[...], preferred_element_type=F32) * INV_ROOT

    def mm_cols(half, s, s_z):
        lhs = [a[:, pl.ds(pl.multiple_of((half + i) * SLOT, SLOT), SLOT)] for i in (s, s_z)]
        lhs = jnp.concatenate(lhs, axis=1)
        return lax.dot_general(lhs, fr[...], TN, preferred_element_type=F32) * INV_ROOT

    pairs_y = (
        (line_y.so, line_y.so_z), (line_y.sp, line_y.sp_z), (line_y.sm, line_y.sm_z), (line_y.own, line_y.own_z),
    )

    for it in range(2):
        dr, dc = (dr0, dc0) if it == 0 else (dr1, dc1)
        rsx = Reduce(line_x, part_r, x_out, x_outz, x_in.at[it], x_inz.at[it], rsx_s.at[it], rsx_r.at[it])
        rsy = Reduce(line_y, part_c, y_out, y_outz, y_in.at[it], y_inz.at[it], rsy_s.at[it], rsy_r.at[it])

        def core_copy(i):
            return pltpu.make_async_remote_copy(
                src_ref=core_out.at[i], dst_ref=core_in.at[it, i],
                send_sem=co_s.at[it, i], recv_sem=co_r.at[it, i],
                device_id=partner, device_id_type=MESH,
            )

        def other_half(i):
            core_out[i] = mm_cols(other_c, *pairs_y[i]).astype(BF16)
            core_copy(i).start()

        def own_half(i):
            value = mm_cols(half_c, *pairs_y[i])
            core_copy(i).wait_recv()
            value = value + core_in[it, i].astype(F32)
            part_of(part_c, pairs_y[i][0])[...] = value[:SLOT]
            part_of(part_c, pairs_y[i][1])[...] = value[SLOT:]

        if it == 0:
            other_half(0)
            other_half(1)
            gy.near()
            gy.far()
            other_half(2)
            other_half(3)
            own_half(0)
            rsy.give(2)
            own_half(1)
            rsy.give(0)
            gy.near_pair()
            gy.far_pair()
            own_half(2)
            rsy.give(1)
            own_half(3)
            gy.from_core()
            mm_rows(line_x.so)
            rsx.give(2)
            mm_rows(line_x.sp)
            rsx.give(0)
            mm_rows(line_x.sm)
            rsx.give(1)
            mm_rows(line_x.own)
        else:
            mm_rows(line_x.so)
            rsx.give(2)
            for i in range(4):
                other_half(i)
            own_half(0)
            rsy.give(2)
            own_half(1)
            rsy.give(0)
            own_half(2)
            rsy.give(1)
            mm_rows(line_x.sp)
            rsx.give(0)
            mm_rows(line_x.sm)
            rsx.give(1)
            own_half(3)
            mm_rows(line_x.own)
        rsy.pair()
        rsx.pair()

        hx = [Gather(line_x, dr, k, agx_s.at[1 + 2 * it + k], agx_r.at[1 + 2 * it + k]) for k in range(2)]
        hy = [
            Gather(line_y, dc, k, agy_s.at[1 + 2 * it + k], agy_r.at[1 + 2 * it + k], half_c, other_c)
            for k in range(2)
        ]
        r0, r1 = part_of(dr, mine_r, 0), part_of(dr, mine_r, 1)
        c0, c1 = part_of(dc, mine_c, 0), part_of(dc, mine_c, 1)
        turn_c = turn(2 + 2 * it, c1, part_of(dr, line_y.own, 1), turn_from)
        turn_r_ = turn(3 + 2 * it, r0, part_of(dc, half_c + col, 0), turn_to)

        if it == 0:

            @pl.when(moves)
            def _():
                turn(1, own1, own_c, turn_from).wait_recv()

        c1[...] = (own_c[...].astype(F32) + rsy.total()).astype(BF16)

        @pl.when(moves)
        def _():
            turn_c.start()

        hy[1].start()
        r0[...] = (own0[...].astype(F32) + rsx.total()).astype(BF16)

        @pl.when(moves)
        def _():
            turn_r_.start()

        hx[0].start()

        @pl.when(stays)
        def _():
            r1[...] = c1[...]
            c0[...] = r0[...]

        hy[1].pair()
        hx[0].pair()

        @pl.when(moves)
        def _():
            turn(2 + 2 * it, r1, r1, turn_to).wait_recv()

        hx[1].start()

        @pl.when(moves)
        def _():
            turn(3 + 2 * it, c0, c0, turn_from).wait_recv()

        hy[0].start()
        hy[1].near()
        hx[0].near()
        hy[1].far()
        hx[0].far()
        hy[1].near_pair()
        hx[0].near_pair()
        hx[1].pair()
        hy[0].pair()
        hy[1].far_pair()
        hx[0].far_pair()
        hy[0].near()
        hx[1].near()
        hy[0].far()
        hx[1].far()
        hy[0].near_pair()
        hx[1].near_pair()
        hy[0].far_pair()
        hx[1].far_pair()
        hy[1].from_core()
        hy[0].from_core()

        if it == 0:

            @pl.loop(0, 4)
            def _(i):
                at_rows = pl.ds(pl.multiple_of(i * 256, 256), 256)
                for j in range(4):
                    cols = slice(j * 512, (j + 1) * 512)
                    residual = lax.dot_general(
                        dr0[at_rows, :], dc0[cols, :], NT, preferred_element_type=F32
                    )
                    den = jnp.concatenate([e_row[at_rows, :]] * 4, axis=1) + e_col[:, cols]
                    a[at_rows, cols] = (-COUPLING * residual / den).astype(BF16)

        for i in range(4):
            core_copy(i).wait_send()
        for exchange in (rsx, rsy, *hx, *hy):
            exchange.sent()

        @pl.when(moves)
        def _():
            turn_c.wait_send()
            turn_r_.wait_send()

    gx.sent()
    gy.sent()

    @pl.when(moves)
    def _():
        turn_f0.wait_send()
        turn_f1.wait_send()


def dma(*shape):
    return pltpu.SemaphoreType.DMA(shape)


def shards(amplitudes, factors, energies):
    row_tile, col_tile = amplitudes.shape
    vmem = pl.BlockSpec(memory_space=pltpu.VMEM)

    def line_buffers():
        return [
            pltpu.VMEM((3, 2, SLOT, K), BF16),
            pltpu.VMEM((SLOT, K), BF16),
            pltpu.VMEM((2, 3, 2, SLOT, K), BF16),
            pltpu.VMEM((2, SLOT, K), BF16),
        ]

    dr, dc = pl.pallas_call(
        cycle,
        out_shape=(
            jax.ShapeDtypeStruct((row_tile, AUX), BF16),
            jax.ShapeDtypeStruct((col_tile, AUX), BF16),
        ),
        in_specs=[pl.BlockSpec(memory_space=pl.ANY), vmem, vmem],
        out_specs=(vmem, vmem),
        scratch_shapes=[
            pltpu.VMEM((row_tile, col_tile), BF16),
            pltpu.VMEM((2, 256, col_tile), F32),
            pltpu.VMEM((row_tile, K), BF16),
            pltpu.VMEM((col_tile, K), BF16),
            pltpu.VMEM((SLOT, K), BF16),
            pltpu.VMEM((row_tile, AUX), BF16),
            pltpu.VMEM((col_tile, AUX), BF16),
            pltpu.VMEM((row_tile, K), F32),
            pltpu.VMEM((row_tile, K), F32),
            pltpu.VMEM((4, 256, K), BF16),
            pltpu.VMEM((2, 4, 256, K), BF16),
            *line_buffers(),
            *line_buffers(),
            pltpu.VMEM((row_tile, 128), F32),
            pltpu.VMEM((1, col_tile), F32),
            dma(2), dma(6), dma(6),
            dma(5, 9), dma(5, 9), dma(5, 17), dma(5, 17),
            dma(2, 7), dma(2, 7), dma(2, 7), dma(2, 7),
            dma(2, 4), dma(2, 4),
        ],
        compiler_params=pltpu.CompilerParams(
            collective_id=0, has_side_effects=True, vmem_limit_bytes=50 * 1024 * 1024
        ),
        name="cycle",
    )(amplitudes, factors, energies.reshape(128, 128))

    row_energy = lax.dynamic_slice_in_dim(energies, lax.axis_index("row") * row_tile, row_tile)
    col_energy = lax.dynamic_slice_in_dim(energies, lax.axis_index("col") * col_tile, col_tile)
    residual = lax.dot_general(dr, dc, NT, preferred_element_type=F32)
    return -COUPLING * residual / (row_energy[:, None] + col_energy[None, :])


def solution(mesh):
    placed = (P("row", "col"), P(("row", "col"), None), P())
    return jax.shard_map(
        shards, mesh=mesh, in_specs=placed, out_specs=P("row", "col"), check_vma=False
    )
```

```python
import functools
import math

import jax
import jax.numpy as jnp
from jax import lax
from jax.experimental import pallas as pl
from jax.experimental.pallas import tpu as pltpu
from jax.sharding import PartitionSpec as P

ORDER = 16384
AUX = 768
COUPLING = ORDER / math.sqrt(AUX)
INV_ROOT = 1.0 / math.sqrt(ORDER)
MESH = pl.DeviceIdType.MESH
BF16, F32 = jnp.bfloat16, jnp.float32

SLOT = 128
HALF = SLOT // 2
K = AUX // 2
NT = (((1,), (1,)), ((), ()))
TN = (((0,), (0,)), ((), ()))


def part_of(ref, slot, k=None, offset=0, size=SLOT):
    rows = pl.ds(pl.multiple_of(slot * SLOT + offset, HALF), size)
    return ref.at[rows, :] if k is None else ref.at[rows, pl.ds(k * K, K)]


class Line:
    def __init__(self, device, slot, core=None):
        self.p, self.m, self.o, self.z = device(1, 0), device(3, 0), device(2, 0), device(0, 1)
        self.core = core
        self.own, self.own_z = slot(0, 0), slot(0, 1)
        self.sp, self.sp_z = slot(1, 0), slot(1, 1)
        self.sm, self.sm_z = slot(3, 0), slot(3, 1)
        self.so, self.so_z = slot(2, 0), slot(2, 1)


class Exchange:
    def __init__(self, send, recv):
        self.send, self.recv = send, recv
        self.started = []

    def copy(self, i, src, dst, target):
        return pltpu.make_async_remote_copy(
            src_ref=src, dst_ref=dst, send_sem=self.send.at[i], recv_sem=self.recv.at[i],
            device_id=target, device_id_type=MESH,
        )

    def go(self, i, src, dst, target):
        c = self.copy(i, src, dst, target)
        c.start()
        self.started.append(c)

    def got(self, i, dst, source):
        self.copy(i, dst, dst, source).wait_recv()

    def sent(self):
        for c in self.started:
            c.wait_send()
        self.started = []


class Gather(Exchange):
    def __init__(self, line, buf, k, send, recv, base=0, other=None, relay_own=False, relay_pair=False):
        super().__init__(send, recv)
        self.line, self.buf, self.k = line, buf, k
        self.base, self.other = base, other
        self.relay_own, self.relay_pair = relay_own, relay_pair

    def view(self, slot, offset=0, size=SLOT):
        return part_of(self.buf, self.base + slot, self.k, offset, size)

    def push(self, i, slot, target, offset=0, size=SLOT, src=None):
        dst = self.view(slot, offset, size)
        self.go(i, dst if src is None else src, dst, target)

    def arrived(self, i, slot, source, offset=0, size=SLOT):
        self.got(i, self.view(slot, offset, size), source)

    def to_core(self, i, slot):
        if self.other is not None:
            self.push(9 + i, slot, self.line.core)

    def start(self, src=None):
        ln = self.line
        self.push(2, ln.own, ln.z, src=src)
        if not self.relay_own:
            self.push(5, ln.own, ln.o, src=src)
        self.push(0, ln.own, ln.p, src=src)
        self.push(1, ln.own, ln.m, src=src)
        self.to_core(0, ln.own)

    def pair(self):
        ln = self.line
        self.arrived(2, ln.own_z, ln.z)
        if not self.relay_pair:
            self.push(7, ln.own_z, ln.o)
        self.push(3, ln.own_z, ln.p)
        self.push(4, ln.own_z, ln.m)
        self.to_core(1, ln.own_z)

    def near(self):
        ln = self.line
        self.arrived(0, ln.sm, ln.m)
        if self.relay_own:
            self.push(5, ln.sm, ln.p, 0, HALF)
        self.to_core(2, ln.sm)
        self.arrived(1, ln.sp, ln.p)
        if self.relay_own:
            self.push(6, ln.sp, ln.m, HALF, HALF)
        self.to_core(3, ln.sp)

    def near_pair(self):
        ln = self.line
        self.arrived(3, ln.sm_z, ln.m)
        if self.relay_pair:
            self.push(7, ln.sm_z, ln.p, 0, HALF)
        self.to_core(4, ln.sm_z)
        self.arrived(4, ln.sp_z, ln.p)
        if self.relay_pair:
            self.push(8, ln.sp_z, ln.m, HALF, HALF)
        self.to_core(5, ln.sp_z)

    def far(self):
        ln = self.line
        if self.relay_own:
            self.arrived(5, ln.so, ln.m, 0, HALF)
            self.arrived(6, ln.so, ln.p, HALF, HALF)
        else:
            self.arrived(5, ln.so, ln.o)
        self.to_core(6, ln.so)

    def far_pair(self):
        ln = self.line
        if self.relay_pair:
            self.arrived(7, ln.so_z, ln.m, 0, HALF)
            self.arrived(8, ln.so_z, ln.p, HALF, HALF)
        else:
            self.arrived(7, ln.so_z, ln.o)
        self.to_core(7, ln.so_z)

    def from_core(self):
        ln = self.line
        order = (ln.own, ln.own_z, ln.sm, ln.sp, ln.sm_z, ln.sp_z, ln.so, ln.so_z)
        for i, slot in enumerate(order):
            self.got(9 + i, part_of(self.buf, self.other + slot, self.k), ln.core)


class Reduce(Exchange):
    def __init__(self, line, part, out, outz, into, inz, send, recv):
        super().__init__(send, recv)
        self.line, self.part = line, part
        self.out, self.outz, self.into, self.inz = out, outz, into, inz

    def give(self, d):
        ln = self.line
        slots, target = (
            ((ln.sp_z, ln.sp), ln.p), ((ln.sm_z, ln.sm), ln.m), ((ln.so_z, ln.so), ln.o),
        )[d]
        for h in range(2):
            self.out[d, h] = part_of(self.part, slots[h])[...].astype(BF16)
            self.go(2 * d + h, self.out.at[d, h], self.into.at[d, h], target)

    def collect(self, h):
        ln = self.line
        for d, source in ((0, ln.m), (1, ln.p), (2, ln.o)):
            self.got(2 * d + h, self.into.at[d, h], source)
        total = part_of(self.part, ln.own if h else ln.own_z)[...]
        for d in range(3):
            total = total + self.into[d, h].astype(F32)
        return total

    def pair(self):
        self.outz[...] = self.collect(0).astype(BF16)
        self.go(6, self.outz, self.inz, self.line.z)

    def total(self):
        total = self.collect(1)
        self.got(6, self.inz, self.line.z)
        return total + self.inz[...].astype(F32)


def spread_energies(energy, e_row, e_col):
    row, col = lax.axis_index("row"), lax.axis_index("col")
    for j in range(8):
        v = energy[pl.ds(row * 8 + j, 1), :]
        e_row[j * 128 : (j + 1) * 128, :] = jnp.broadcast_to(v, (128, 128)).T
    for j in range(16):
        e_col[:, j * 128 : (j + 1) * 128] = energy[pl.ds(col * 16 + j, 1), :]


def tile(dr, dc, e_row, e_col, rows, cols):
    residual = lax.dot_general(dr[rows, :], dc[cols, :], NT, preferred_element_type=F32)
    den = jnp.concatenate([e_row[rows, :]] * (residual.shape[1] // 128), axis=1) + e_col[:, cols]
    return -COUPLING * residual / den


def finish(dr, dc, energy, out, stage, e_row, e_col, sem):
    spread_energies(energy, e_row, e_col)

    def put(i):
        return pltpu.make_async_copy(stage.at[i % 2], out.at[pl.ds(i * 128, 128), :], sem.at[i % 2])

    for i in range(8):
        if i >= 2:
            put(i - 2).wait()
        for j in range(4):
            cols = slice(j * 512, (j + 1) * 512)
            stage[i % 2, :, cols] = tile(dr, dc, e_row, e_col, slice(i * 128, (i + 1) * 128), cols)
        put(i).start()
    put(6).wait()
    put(7).wait()


def cycle(
    amp, own, energy, dr1, dc1,
    a, stage, fr, fc, own_c, dr0, dc0, part_r, part_c, core_out, core_in,
    x_out, x_outz, x_in, x_inz, y_out, y_outz, y_in, y_inz,
    e_row, e_col,
    amp_sem, turn_s, turn_r, agx_s, agx_r, agy_s, agy_r, rsx_s, rsx_r, rsy_s, rsy_r, co_s, co_r,
):
    row, col = lax.axis_index("row"), lax.axis_index("col")
    core, chip_row = lax.rem(row, 2), row // 2
    hi, y = chip_row // 4, lax.rem(chip_row, 4)
    x, lo = col // 2, lax.rem(col, 2)

    def at(r, c):
        return {"row": r, "col": c}

    def x_slot(step, flip):
        return lax.rem(x + step, 4) * 2 + (1 - lo if flip else lo)

    first_y = lax.rem(x, 2) * 2 + lo
    parity = x // 2 + lo

    def y_slot(step, flip):
        z = 1 - hi if flip else hi
        return lax.rem(x + y + step + 4 - first_y, 4) * 2 + lax.rem(z + parity, 2)

    def dev_x(step, flip):
        return at(row, x_slot(step, flip))

    def dev_y(step, flip):
        z = 1 - hi if flip else hi
        return at((z * 4 + lax.rem(y + step, 4)) * 2 + core, col)

    partner = at(chip_row * 2 + 1 - core, col)
    line_x = Line(dev_x, x_slot)
    line_y = Line(dev_y, y_slot, partner)

    x_to = chip_row // 2
    y_to = lax.rem(y + x + 4 - x_to, 4)
    hi_to = lax.rem(hi + lo + y, 2)
    to_row, to_col = (hi_to * 4 + y_to) * 2 + core, x_to * 2 + lax.rem(y, 2)
    turn_to = at(to_row, to_col)
    turn_from = at(col * 2 + core, line_y.own)
    moves = (to_row - row) * (to_row - row) + (to_col - col) * (to_col - col) != 0
    stays = jnp.logical_not(moves)

    half_c, other_c = core * 8, (1 - core) * 8
    mine_r, mine_c = line_x.own, half_c + line_y.own

    def turn(i, src, dst, device):
        return pltpu.make_async_remote_copy(
            src_ref=src, dst_ref=dst, send_sem=turn_s.at[i], recv_sem=turn_r.at[i],
            device_id=device, device_id_type=MESH,
        )

    def amp_copy(i):
        return pltpu.make_async_copy(amp.at[pl.ds(i * 256, 256), :], stage.at[i % 2], amp_sem.at[i % 2])

    amp_copy(0).start()
    amp_copy(1).start()

    barrier = pltpu.get_barrier_semaphore()

    def greet(device):
        pl.semaphore_signal(barrier, inc=1, device_id=device, device_id_type=MESH)

    for ln in (line_x, line_y):
        for device in (ln.p, ln.m, ln.o, ln.z):
            greet(device)
    greet(partner)

    @pl.when(moves)
    def _():
        greet(turn_to)
        greet(turn_from)

    spread_energies(energy, e_row, e_col)

    @pl.when(moves)
    def _():
        pl.semaphore_wait(barrier, 11)

    @pl.when(stays)
    def _():
        pl.semaphore_wait(barrier, 9)

    gx = Gather(line_x, fr, None, agx_s.at[0], agx_r.at[0])
    gy = Gather(line_y, fc, None, agy_s.at[0], agy_r.at[0], half_c, other_c)
    own0, own1 = own.at[:, pl.ds(0, K)], own.at[:, pl.ds(K, K)]
    turn_f0 = turn(0, own0, part_of(fc, half_c + col), turn_to)
    turn_f1 = turn(1, own1, own_c, turn_to)

    @pl.when(moves)
    def _():
        turn_f0.start()

    gx.start(src=own1)

    @pl.when(moves)
    def _():
        turn_f1.start()

    part_of(fr, mine_r)[...] = own1[...]

    @pl.when(stays)
    def _():
        part_of(fc, mine_c)[...] = own0[...]
        own_c[...] = own1[...]

    for i in range(4):
        amp_copy(i).wait()
        a[i * 256 : (i + 1) * 256, :] = stage[i % 2].astype(BF16)
        if i + 2 < 4:
            amp_copy(i + 2).start()

    gx.pair()

    @pl.when(moves)
    def _():
        turn(0, own0, part_of(fc, mine_c), turn_from).wait_recv()

    gy.start()
    gx.near()
    gx.far()
    gy.pair()
    gx.near_pair()
    gx.far_pair()

    def mm_rows(s):
        at_rows = pl.ds(pl.multiple_of((s // 2) * 256, 256), 256)
        part_r[at_rows, :] = jnp.dot(a[at_rows, :], fc[...], preferred_element_type=F32) * INV_ROOT

    def mm_cols(half, s, s_z):
        lhs = [a[:, pl.ds(pl.multiple_of((half + i) * SLOT, SLOT), SLOT)] for i in (s, s_z)]
        lhs = jnp.concatenate(lhs, axis=1)
        return lax.dot_general(lhs, fr[...], TN, preferred_element_type=F32) * INV_ROOT

    pairs_y = (
        (line_y.so, line_y.so_z), (line_y.sp, line_y.sp_z), (line_y.sm, line_y.sm_z), (line_y.own, line_y.own_z),
    )

    for it in range(2):
        dr, dc = (dr0, dc0) if it == 0 else (dr1, dc1)
        rsx = Reduce(line_x, part_r, x_out, x_outz, x_in.at[it], x_inz.at[it], rsx_s.at[it], rsx_r.at[it])
        rsy = Reduce(line_y, part_c, y_out, y_outz, y_in.at[it], y_inz.at[it], rsy_s.at[it], rsy_r.at[it])

        def core_copy(i):
            return pltpu.make_async_remote_copy(
                src_ref=core_out.at[i], dst_ref=core_in.at[it, i],
                send_sem=co_s.at[it, i], recv_sem=co_r.at[it, i],
                device_id=partner, device_id_type=MESH,
            )

        def other_half(i):
            core_out[i] = mm_cols(other_c, *pairs_y[i]).astype(BF16)
            core_copy(i).start()

        def own_half(i):
            value = mm_cols(half_c, *pairs_y[i])
            core_copy(i).wait_recv()
            value = value + core_in[it, i].astype(F32)
            part_of(part_c, pairs_y[i][0])[...] = value[:SLOT]
            part_of(part_c, pairs_y[i][1])[...] = value[SLOT:]

        if it == 0:
            other_half(0)
            other_half(1)
            gy.near()
            gy.far()
            other_half(2)
            other_half(3)
            own_half(0)
            rsy.give(2)
            own_half(1)
            rsy.give(0)
            gy.near_pair()
            gy.far_pair()
            own_half(2)
            rsy.give(1)
            own_half(3)
            gy.from_core()
            mm_rows(line_x.so)
            rsx.give(2)
            mm_rows(line_x.sp)
            rsx.give(0)
            mm_rows(line_x.sm)
            rsx.give(1)
            mm_rows(line_x.own)
        else:
            mm_rows(line_x.so)
            rsx.give(2)
            for i in range(4):
                other_half(i)
            own_half(0)
            rsy.give(2)
            own_half(1)
            rsy.give(0)
            own_half(2)
            rsy.give(1)
            mm_rows(line_x.sp)
            rsx.give(0)
            mm_rows(line_x.sm)
            rsx.give(1)
            own_half(3)
            mm_rows(line_x.own)
        rsy.pair()
        rsx.pair()

        hx = [
            Gather(
                line_x, dr, k, agx_s.at[1 + 2 * it + k], agx_r.at[1 + 2 * it + k],
                relay_own=True, relay_pair=k == 0,
            )
            for k in range(2)
        ]
        hy = [
            Gather(
                line_y, dc, k, agy_s.at[1 + 2 * it + k], agy_r.at[1 + 2 * it + k], half_c, other_c,
                relay_own=True, relay_pair=k == 1,
            )
            for k in range(2)
        ]
        r0, r1 = part_of(dr, mine_r, 0), part_of(dr, mine_r, 1)
        c0, c1 = part_of(dc, mine_c, 0), part_of(dc, mine_c, 1)
        turn_c = turn(2 + 2 * it, c1, part_of(dr, line_y.own, 1), turn_from)
        turn_r_ = turn(3 + 2 * it, r0, part_of(dc, half_c + col, 0), turn_to)

        if it == 0:

            @pl.when(moves)
            def _():
                turn(1, own1, own_c, turn_from).wait_recv()

        c1[...] = (own_c[...].astype(F32) + rsy.total()).astype(BF16)

        @pl.when(moves)
        def _():
            turn_c.start()

        hy[1].start()
        r0[...] = (own0[...].astype(F32) + rsx.total()).astype(BF16)

        @pl.when(moves)
        def _():
            turn_r_.start()

        hx[0].start()

        @pl.when(stays)
        def _():
            r1[...] = c1[...]
            c0[...] = r0[...]

        hy[1].pair()
        hx[0].pair()

        @pl.when(moves)
        def _():
            turn(2 + 2 * it, r1, r1, turn_to).wait_recv()

        hx[1].start()

        @pl.when(moves)
        def _():
            turn(3 + 2 * it, c0, c0, turn_from).wait_recv()

        hy[0].start()
        hy[1].near()
        hx[0].near()
        hy[1].near_pair()
        hx[0].near_pair()
        hy[0].pair()
        hx[1].pair()
        hy[1].far()
        hx[0].far()
        hy[0].near()
        hx[1].near()
        hy[1].far_pair()
        hx[0].far_pair()
        hy[0].near_pair()
        hx[1].near_pair()
        hy[0].far()
        hx[1].far()
        hy[0].far_pair()
        hx[1].far_pair()
        hy[1].from_core()
        hy[0].from_core()

        if it == 0:

            @pl.loop(0, 4)
            def _(i):
                at_rows = pl.ds(pl.multiple_of(i * 256, 256), 256)
                for j in range(4):
                    cols = slice(j * 512, (j + 1) * 512)
                    a[at_rows, cols] = tile(dr0, dc0, e_row, e_col, at_rows, cols).astype(BF16)

        for i in range(4):
            core_copy(i).wait_send()
        for exchange in (rsx, rsy, *hx, *hy):
            exchange.sent()

        @pl.when(moves)
        def _():
            turn_c.wait_send()
            turn_r_.wait_send()

    gx.sent()
    gy.sent()

    @pl.when(moves)
    def _():
        turn_f0.wait_send()
        turn_f1.wait_send()


def dma(*shape):
    return pltpu.SemaphoreType.DMA(shape)


def shards(amplitudes, factors, energies):
    row_tile, col_tile = amplitudes.shape
    vmem = pl.BlockSpec(memory_space=pltpu.VMEM)

    def line_buffers():
        return [
            pltpu.VMEM((3, 2, SLOT, K), BF16),
            pltpu.VMEM((SLOT, K), BF16),
            pltpu.VMEM((2, 3, 2, SLOT, K), BF16),
            pltpu.VMEM((2, SLOT, K), BF16),
        ]

    energy = energies.reshape(128, 128)
    dr, dc = pl.pallas_call(
        cycle,
        out_shape=(
            jax.ShapeDtypeStruct((row_tile, AUX), BF16),
            jax.ShapeDtypeStruct((col_tile, AUX), BF16),
        ),
        in_specs=[pl.BlockSpec(memory_space=pl.ANY), vmem, vmem],
        out_specs=(vmem, vmem),
        scratch_shapes=[
            pltpu.VMEM((row_tile, col_tile), BF16),
            pltpu.VMEM((2, 256, col_tile), F32),
            pltpu.VMEM((row_tile, K), BF16),
            pltpu.VMEM((col_tile, K), BF16),
            pltpu.VMEM((SLOT, K), BF16),
            pltpu.VMEM((row_tile, AUX), BF16),
            pltpu.VMEM((col_tile, AUX), BF16),
            pltpu.VMEM((row_tile, K), F32),
            pltpu.VMEM((row_tile, K), F32),
            pltpu.VMEM((4, 256, K), BF16),
            pltpu.VMEM((2, 4, 256, K), BF16),
            *line_buffers(),
            *line_buffers(),
            pltpu.VMEM((row_tile, 128), F32),
            pltpu.VMEM((1, col_tile), F32),
            dma(2), dma(6), dma(6),
            dma(5, 9), dma(5, 9), dma(5, 17), dma(5, 17),
            dma(2, 7), dma(2, 7), dma(2, 7), dma(2, 7),
            dma(2, 4), dma(2, 4),
        ],
        compiler_params=pltpu.CompilerParams(
            collective_id=0, has_side_effects=True, vmem_limit_bytes=46 * 1024 * 1024
        ),
        name="cycle",
    )(amplitudes, factors, energy)

    return pl.pallas_call(
        finish,
        out_shape=jax.ShapeDtypeStruct((row_tile, col_tile), F32),
        in_specs=[vmem, vmem, vmem],
        out_specs=pl.BlockSpec(memory_space=pl.ANY),
        scratch_shapes=[
            pltpu.VMEM((2, 128, col_tile), F32),
            pltpu.VMEM((row_tile, 128), F32),
            pltpu.VMEM((1, col_tile), F32),
            dma(2),
        ],
        compiler_params=pltpu.CompilerParams(vmem_limit_bytes=20 * 1024 * 1024),
        name="finish",
    )(dr, dc, energy)


def solution(mesh):
    placed = (P("row", "col"), P(("row", "col"), None), P())
    return jax.shard_map(
        shards, mesh=mesh, in_specs=placed, out_specs=P("row", "col"), check_vma=False
    )
```

```python
import functools
import math

import jax
import jax.numpy as jnp
from jax import lax
from jax.experimental import pallas as pl
from jax.experimental.pallas import tpu as pltpu
from jax.sharding import PartitionSpec as P

ORDER = 16384
AUX = 768
COUPLING = ORDER / math.sqrt(AUX)
INV_ROOT = 1.0 / math.sqrt(ORDER)
MESH = pl.DeviceIdType.MESH
BF16, F32 = jnp.bfloat16, jnp.float32

SLOT = 128
HALF = SLOT // 2
K = AUX // 2
NT = (((1,), (1,)), ((), ()))
TN = (((0,), (0,)), ((), ()))


def part_of(ref, slot, k=None, offset=0, size=SLOT):
    rows = pl.ds(pl.multiple_of(slot * SLOT + offset, HALF), size)
    return ref.at[rows, :] if k is None else ref.at[rows, pl.ds(k * K, K)]


class Line:
    def __init__(self, device, slot, core=None):
        self.p, self.m, self.o, self.z = device(1, 0), device(3, 0), device(2, 0), device(0, 1)
        self.core = core
        self.own, self.own_z = slot(0, 0), slot(0, 1)
        self.sp, self.sp_z = slot(1, 0), slot(1, 1)
        self.sm, self.sm_z = slot(3, 0), slot(3, 1)
        self.so, self.so_z = slot(2, 0), slot(2, 1)


class Exchange:
    def __init__(self, send, recv):
        self.send, self.recv = send, recv
        self.started = []

    def copy(self, i, src, dst, target):
        return pltpu.make_async_remote_copy(
            src_ref=src, dst_ref=dst, send_sem=self.send.at[i], recv_sem=self.recv.at[i],
            device_id=target, device_id_type=MESH,
        )

    def go(self, i, src, dst, target):
        c = self.copy(i, src, dst, target)
        c.start()
        self.started.append(c)

    def got(self, i, dst, source):
        self.copy(i, dst, dst, source).wait_recv()

    def sent(self):
        for c in self.started:
            c.wait_send()
        self.started = []


class Gather(Exchange):
    def __init__(self, line, buf, k, send, recv, base=0, other=None, relay_own=False, relay_pair=False):
        super().__init__(send, recv)
        self.line, self.buf, self.k = line, buf, k
        self.base, self.other = base, other
        self.relay_own, self.relay_pair = relay_own, relay_pair

    def view(self, slot, offset=0, size=SLOT):
        return part_of(self.buf, self.base + slot, self.k, offset, size)

    def push(self, i, slot, target, offset=0, size=SLOT, src=None):
        dst = self.view(slot, offset, size)
        self.go(i, dst if src is None else src, dst, target)

    def arrived(self, i, slot, source, offset=0, size=SLOT):
        self.got(i, self.view(slot, offset, size), source)

    def to_core(self, i, slot):
        if self.other is not None:
            self.push(9 + i, slot, self.line.core)

    def start(self, src=None):
        ln = self.line
        self.push(2, ln.own, ln.z, src=src)
        if not self.relay_own:
            self.push(5, ln.own, ln.o, src=src)
        self.push(0, ln.own, ln.p, src=src)
        self.push(1, ln.own, ln.m, src=src)
        self.to_core(0, ln.own)

    def pair(self):
        ln = self.line
        self.arrived(2, ln.own_z, ln.z)
        if not self.relay_pair:
            self.push(7, ln.own_z, ln.o)
        self.push(3, ln.own_z, ln.p)
        self.push(4, ln.own_z, ln.m)
        self.to_core(1, ln.own_z)

    def near(self):
        ln = self.line
        self.arrived(0, ln.sm, ln.m)
        if self.relay_own:
            self.push(5, ln.sm, ln.p, 0, HALF)
        self.to_core(2, ln.sm)
        self.arrived(1, ln.sp, ln.p)
        if self.relay_own:
            self.push(6, ln.sp, ln.m, HALF, HALF)
        self.to_core(3, ln.sp)

    def near_pair(self):
        ln = self.line
        self.arrived(3, ln.sm_z, ln.m)
        if self.relay_pair:
            self.push(7, ln.sm_z, ln.p, 0, HALF)
        self.to_core(4, ln.sm_z)
        self.arrived(4, ln.sp_z, ln.p)
        if self.relay_pair:
            self.push(8, ln.sp_z, ln.m, HALF, HALF)
        self.to_core(5, ln.sp_z)

    def far(self):
        ln = self.line
        if self.relay_own:
            self.arrived(5, ln.so, ln.m, 0, HALF)
            self.arrived(6, ln.so, ln.p, HALF, HALF)
        else:
            self.arrived(5, ln.so, ln.o)
        self.to_core(6, ln.so)

    def far_pair(self):
        ln = self.line
        if self.relay_pair:
            self.arrived(7, ln.so_z, ln.m, 0, HALF)
            self.arrived(8, ln.so_z, ln.p, HALF, HALF)
        else:
            self.arrived(7, ln.so_z, ln.o)
        self.to_core(7, ln.so_z)

    def from_core(self, first=0, last=8):
        ln = self.line
        order = (ln.own, ln.own_z, ln.sm, ln.sp, ln.sm_z, ln.sp_z, ln.so, ln.so_z)
        for i in range(first, last):
            self.got(9 + i, part_of(self.buf, self.other + order[i], self.k), ln.core)


class Reduce(Exchange):
    def __init__(self, line, part, out, outz, into, inz, send, recv):
        super().__init__(send, recv)
        self.line, self.part = line, part
        self.out, self.outz, self.into, self.inz = out, outz, into, inz

    def give(self, d):
        ln = self.line
        slots, target = (
            ((ln.sp_z, ln.sp), ln.p), ((ln.sm_z, ln.sm), ln.m), ((ln.so_z, ln.so), ln.o),
        )[d]
        for h in range(2):
            self.out[d, h] = part_of(self.part, slots[h])[...].astype(BF16)
            self.go(2 * d + h, self.out.at[d, h], self.into.at[d, h], target)

    def collect(self, h):
        ln = self.line
        for d, source in ((0, ln.m), (1, ln.p), (2, ln.o)):
            self.got(2 * d + h, self.into.at[d, h], source)
        total = part_of(self.part, ln.own if h else ln.own_z)[...]
        for d in range(3):
            total = total + self.into[d, h].astype(F32)
        return total

    def pair(self):
        self.outz[...] = self.collect(0).astype(BF16)
        self.go(6, self.outz, self.inz, self.line.z)

    def total(self):
        total = self.collect(1)
        self.got(6, self.inz, self.line.z)
        return total + self.inz[...].astype(F32)


def spread_energies(energy, e_row, e_col):
    row, col = lax.axis_index("row"), lax.axis_index("col")
    for j in range(8):
        v = energy[pl.ds(row * 8 + j, 1), :]
        e_row[j * 128 : (j + 1) * 128, :] = jnp.broadcast_to(v, (128, 128)).T
    for j in range(16):
        e_col[:, j * 128 : (j + 1) * 128] = energy[pl.ds(col * 16 + j, 1), :]


def tile(dr, dc, e_row, e_col):
    residual = lax.dot_general(dr, dc, NT, preferred_element_type=F32)
    den = jnp.concatenate([e_row] * (residual.shape[1] // 128), axis=1) + e_col
    return -COUPLING * residual / den


def finish(dr, dc, e_row, e_col, out, stage, sem):
    def put(i):
        return pltpu.make_async_copy(stage.at[i % 2], out.at[pl.ds(i * 256, 256), :], sem.at[i % 2])

    for i in range(4):
        if i >= 2:
            put(i - 2).wait()
        for j in range(4):
            cols = slice(j * 512, (j + 1) * 512)
            rows = slice(i * 256, (i + 1) * 256)
            stage[i % 2, :, cols] = tile(dr[rows, :], dc[cols, :], e_row[rows, :], e_col[:, cols])
        put(i).start()
    put(2).wait()
    put(3).wait()


def cycle(
    amp, own_hbm, energy_hbm, dr1, dc1, e_row, e_col,
    a, stage, own, energy, fr, fc, own_c, dr0, dc0, part_r, part_c, core_out, core_in,
    x_out, x_outz, x_in, x_inz, y_out, y_outz, y_in, y_inz,
    amp_sem, in_sem, turn_s, turn_r, agx_s, agx_r, agy_s, agy_r, rsx_s, rsx_r, rsy_s, rsy_r, co_s, co_r,
):
    row, col = lax.axis_index("row"), lax.axis_index("col")
    core, chip_row = lax.rem(row, 2), row // 2
    hi, y = chip_row // 4, lax.rem(chip_row, 4)
    x, lo = col // 2, lax.rem(col, 2)

    def at(r, c):
        return {"row": r, "col": c}

    def x_slot(step, flip):
        return lax.rem(x + step, 4) * 2 + (1 - lo if flip else lo)

    first_y = lax.rem(x, 2) * 2 + lo
    parity = x // 2 + lo

    def y_slot(step, flip):
        z = 1 - hi if flip else hi
        return lax.rem(x + y + step + 4 - first_y, 4) * 2 + lax.rem(z + parity, 2)

    def dev_x(step, flip):
        return at(row, x_slot(step, flip))

    def dev_y(step, flip):
        z = 1 - hi if flip else hi
        return at((z * 4 + lax.rem(y + step, 4)) * 2 + core, col)

    partner = at(chip_row * 2 + 1 - core, col)
    line_x = Line(dev_x, x_slot)
    line_y = Line(dev_y, y_slot, partner)

    x_to = chip_row // 2
    y_to = lax.rem(y + x + 4 - x_to, 4)
    hi_to = lax.rem(hi + lo + y, 2)
    to_row, to_col = (hi_to * 4 + y_to) * 2 + core, x_to * 2 + lax.rem(y, 2)
    turn_to = at(to_row, to_col)
    turn_from = at(col * 2 + core, line_y.own)
    moves = (to_row - row) * (to_row - row) + (to_col - col) * (to_col - col) != 0
    stays = jnp.logical_not(moves)

    half_c, other_c = core * 8, (1 - core) * 8
    mine_r, mine_c = line_x.own, half_c + line_y.own

    def turn(i, src, dst, device):
        return pltpu.make_async_remote_copy(
            src_ref=src, dst_ref=dst, send_sem=turn_s.at[i], recv_sem=turn_r.at[i],
            device_id=device, device_id_type=MESH,
        )

    def amp_copy(i):
        return pltpu.make_async_copy(amp.at[pl.ds(i * 256, 256), :], stage.at[i % 2], amp_sem.at[i % 2])

    own_copy = pltpu.make_async_copy(own_hbm, own, in_sem.at[0])
    energy_copy = pltpu.make_async_copy(energy_hbm, energy, in_sem.at[1])
    own_copy.start()
    energy_copy.start()
    amp_copy(0).start()
    amp_copy(1).start()

    barrier = pltpu.get_barrier_semaphore()

    def greet(device):
        pl.semaphore_signal(barrier, inc=1, device_id=device, device_id_type=MESH)

    for ln in (line_x, line_y):
        for device in (ln.p, ln.m, ln.o, ln.z):
            greet(device)
    greet(partner)

    @pl.when(moves)
    def _():
        greet(turn_to)
        greet(turn_from)

    own_copy.wait()

    @pl.when(moves)
    def _():
        pl.semaphore_wait(barrier, 11)

    @pl.when(stays)
    def _():
        pl.semaphore_wait(barrier, 9)

    gx = Gather(line_x, fr, None, agx_s.at[0], agx_r.at[0], relay_own=True)
    gy = Gather(line_y, fc, None, agy_s.at[0], agy_r.at[0], half_c, other_c, relay_own=True)
    own0, own1 = own.at[:, pl.ds(0, K)], own.at[:, pl.ds(K, K)]
    turn_f0 = turn(0, own0, part_of(fc, half_c + col), turn_to)
    turn_f1 = turn(1, own1, own_c, turn_to)

    @pl.when(moves)
    def _():
        turn_f0.start()

    gx.start(src=own1)

    @pl.when(moves)
    def _():
        turn_f1.start()

    part_of(fr, mine_r)[...] = own1[...]

    @pl.when(stays)
    def _():
        part_of(fc, mine_c)[...] = own0[...]
        own_c[...] = own1[...]

    energy_copy.wait()
    spread_energies(energy, e_row, e_col)
    for i in range(4):
        amp_copy(i).wait()
        a[i * 256 : (i + 1) * 256, :] = stage[i % 2].astype(BF16)
        if i + 2 < 4:
            amp_copy(i + 2).start()

    gx.pair()

    @pl.when(moves)
    def _():
        turn(0, own0, part_of(fc, mine_c), turn_from).wait_recv()

    gy.start()
    gx.near()
    gy.pair()
    gx.near_pair()
    gx.far()
    gy.near()
    gx.far_pair()

    def mm_rows(s):
        at_rows = pl.ds(pl.multiple_of((s // 2) * 256, 256), 256)
        part_r[at_rows, :] = jnp.dot(a[at_rows, :], fc[...], preferred_element_type=F32) * INV_ROOT

    def mm_cols(half, s, s_z):
        lhs = [a[:, pl.ds(pl.multiple_of((half + i) * SLOT, SLOT), SLOT)] for i in (s, s_z)]
        lhs = jnp.concatenate(lhs, axis=1)
        return lax.dot_general(lhs, fr[...], TN, preferred_element_type=F32) * INV_ROOT

    def new_tile(i, j):
        rows = pl.ds(pl.multiple_of(lax.rem(x + i, 4) * 256, 256), 256)
        first = lax.rem(x + y + j + 4 - first_y, 4) * 256
        cols = [pl.ds(pl.multiple_of(h * 1024 + first, 256), 256) for h in range(2)]
        value = tile(
            dr0[rows, :],
            jnp.concatenate([dc0[c, :] for c in cols], axis=0),
            e_row[rows, :],
            jnp.concatenate([e_col[:, c] for c in cols], axis=1),
        ).astype(BF16)
        for h in range(2):
            a[rows, cols[h]] = value[:, h * 256 : (h + 1) * 256]

    def new_tiles(t):
        @pl.loop(0, 3)
        def _(n):
            new_tile(t + t // 2, n + n // 2)

    pairs_y = (
        (line_y.so, line_y.so_z), (line_y.sp, line_y.sp_z), (line_y.sm, line_y.sm_z), (line_y.own, line_y.own_z),
    )

    for it in range(2):
        dr, dc = (dr0, dc0) if it == 0 else (dr1, dc1)
        rsx = Reduce(line_x, part_r, x_out, x_outz, x_in.at[it], x_inz.at[it], rsx_s.at[it], rsx_r.at[it])
        rsy = Reduce(line_y, part_c, y_out, y_outz, y_in.at[it], y_inz.at[it], rsy_s.at[it], rsy_r.at[it])

        def core_copy(i):
            return pltpu.make_async_remote_copy(
                src_ref=core_out.at[i], dst_ref=core_in.at[it, i],
                send_sem=co_s.at[it, i], recv_sem=co_r.at[it, i],
                device_id=partner, device_id_type=MESH,
            )

        def other_half(i):
            core_out[i] = mm_cols(other_c, *pairs_y[i]).astype(BF16)
            core_copy(i).start()

        def own_half(i):
            value = mm_cols(half_c, *pairs_y[i])
            core_copy(i).wait_recv()
            value = value + core_in[it, i].astype(F32)
            part_of(part_c, pairs_y[i][0])[...] = value[:SLOT]
            part_of(part_c, pairs_y[i][1])[...] = value[SLOT:]

        if it == 0:
            other_half(0)
            other_half(1)
            gy.near_pair()
            other_half(2)
            other_half(3)
            own_half(0)
            rsy.give(2)
            own_half(1)
            rsy.give(0)
            gy.far()
            gy.far_pair()
            own_half(2)
            rsy.give(1)
            own_half(3)
            gy.from_core()
            mm_rows(line_x.so)
            rsx.give(2)
            mm_rows(line_x.sp)
            rsx.give(0)
            mm_rows(line_x.sm)
            rsx.give(1)
            mm_rows(line_x.own)
        else:
            mm_rows(line_x.so)
            rsx.give(2)
            for i in range(4):
                other_half(i)
            own_half(0)
            rsy.give(2)
            own_half(1)
            rsy.give(0)
            own_half(2)
            rsy.give(1)
            mm_rows(line_x.sp)
            rsx.give(0)
            mm_rows(line_x.sm)
            rsx.give(1)
            own_half(3)
            mm_rows(line_x.own)
        rsy.pair()
        rsx.pair()

        hx = [
            Gather(
                line_x, dr, k, agx_s.at[1 + 2 * it + k], agx_r.at[1 + 2 * it + k],
                relay_own=True, relay_pair=k == 0,
            )
            for k in range(2)
        ]
        hy = [
            Gather(
                line_y, dc, k, agy_s.at[1 + 2 * it + k], agy_r.at[1 + 2 * it + k], half_c, other_c,
                relay_own=True, relay_pair=k == 1,
            )
            for k in range(2)
        ]
        r0, r1 = part_of(dr, mine_r, 0), part_of(dr, mine_r, 1)
        c0, c1 = part_of(dc, mine_c, 0), part_of(dc, mine_c, 1)
        turn_c = turn(2 + 2 * it, c1, part_of(dr, line_y.own, 1), turn_from)
        turn_r_ = turn(3 + 2 * it, r0, part_of(dc, half_c + col, 0), turn_to)

        if it == 0:

            @pl.when(moves)
            def _():
                turn(1, own1, own_c, turn_from).wait_recv()

        c1[...] = (own_c[...].astype(F32) + rsy.total()).astype(BF16)

        @pl.when(moves)
        def _():
            turn_c.start()

        hy[1].start()
        r0[...] = (own0[...].astype(F32) + rsx.total()).astype(BF16)

        @pl.when(moves)
        def _():
            turn_r_.start()

        hx[0].start()

        @pl.when(stays)
        def _():
            r1[...] = c1[...]
            c0[...] = r0[...]

        hy[1].pair()
        hx[0].pair()

        @pl.when(moves)
        def _():
            turn(2 + 2 * it, r1, r1, turn_to).wait_recv()

        hx[1].start()

        @pl.when(moves)
        def _():
            turn(3 + 2 * it, c0, c0, turn_from).wait_recv()

        hy[0].start()
        hy[1].near()
        hx[0].near()
        hy[1].near_pair()
        hx[0].near_pair()
        hy[0].pair()
        hx[1].pair()
        hy[1].far()
        hx[0].far()
        hy[0].near()
        hx[1].near()
        hy[1].far_pair()
        hx[0].far_pair()
        hy[0].near_pair()
        hx[1].near_pair()
        if it == 0:
            hy[1].from_core()
            hy[0].from_core(0, 6)
            new_tiles(0)
            hy[0].far()
            hx[1].far()
            new_tiles(1)
            hy[0].far_pair()
            hx[1].far_pair()
            new_tiles(2)
            hy[0].from_core(6, 8)

            @pl.loop(0, 4)
            def _(n):
                new_tile(2, n)

            @pl.loop(0, 3)
            def _(n):
                new_tile(n + n // 2, 2)
        else:
            hy[0].far()
            hx[1].far()
            hy[0].far_pair()
            hx[1].far_pair()
            hy[1].from_core()
            hy[0].from_core()

        for i in range(4):
            core_copy(i).wait_send()
        for exchange in (rsx, rsy, *hx, *hy):
            exchange.sent()

        @pl.when(moves)
        def _():
            turn_c.wait_send()
            turn_r_.wait_send()

    gx.sent()
    gy.sent()

    @pl.when(moves)
    def _():
        turn_f0.wait_send()
        turn_f1.wait_send()


def dma(*shape):
    return pltpu.SemaphoreType.DMA(shape)


def shards(amplitudes, factors, energies):
    row_tile, col_tile = amplitudes.shape
    vmem = pl.BlockSpec(memory_space=pltpu.VMEM)

    def line_buffers():
        return [
            pltpu.VMEM((3, 2, SLOT, K), BF16),
            pltpu.VMEM((SLOT, K), BF16),
            pltpu.VMEM((2, 3, 2, SLOT, K), BF16),
            pltpu.VMEM((2, SLOT, K), BF16),
        ]

    energy = energies.reshape(128, 128)
    hbm = pl.BlockSpec(memory_space=pltpu.MemorySpace.HBM)
    dr, dc, e_row, e_col = pl.pallas_call(
        cycle,
        out_shape=(
            jax.ShapeDtypeStruct((row_tile, AUX), BF16),
            jax.ShapeDtypeStruct((col_tile, AUX), BF16),
            jax.ShapeDtypeStruct((row_tile, 128), F32),
            jax.ShapeDtypeStruct((1, col_tile), F32),
        ),
        in_specs=[hbm, hbm, hbm],
        out_specs=(vmem, vmem, vmem, vmem),
        scratch_shapes=[
            pltpu.VMEM((row_tile, col_tile), BF16),
            pltpu.VMEM((2, 256, col_tile), F32),
            pltpu.VMEM((SLOT, AUX), BF16),
            pltpu.VMEM((128, 128), F32),
            pltpu.VMEM((row_tile, K), BF16),
            pltpu.VMEM((col_tile, K), BF16),
            pltpu.VMEM((SLOT, K), BF16),
            pltpu.VMEM((row_tile, AUX), BF16),
            pltpu.VMEM((col_tile, AUX), BF16),
            pltpu.VMEM((row_tile, K), F32),
            pltpu.VMEM((row_tile, K), F32),
            pltpu.VMEM((4, 256, K), BF16),
            pltpu.VMEM((2, 4, 256, K), BF16),
            *line_buffers(),
            *line_buffers(),
            dma(2), dma(2), dma(6), dma(6),
            dma(5, 9), dma(5, 9), dma(5, 17), dma(5, 17),
            dma(2, 7), dma(2, 7), dma(2, 7), dma(2, 7),
            dma(2, 4), dma(2, 4),
        ],
        compiler_params=pltpu.CompilerParams(
            collective_id=0, has_side_effects=True, vmem_limit_bytes=46 * 1024 * 1024
        ),
        name="cycle",
    )(*(pltpu.with_memory_space_constraint(v, pltpu.MemorySpace.HBM) for v in (amplitudes, factors, energy)))

    return pl.pallas_call(
        finish,
        out_shape=jax.ShapeDtypeStruct((row_tile, col_tile), F32),
        in_specs=[vmem, vmem, vmem, vmem],
        out_specs=pl.BlockSpec(memory_space=pl.ANY),
        scratch_shapes=[pltpu.VMEM((2, 256, col_tile), F32), dma(2)],
        compiler_params=pltpu.CompilerParams(vmem_limit_bytes=20 * 1024 * 1024),
        name="finish",
    )(dr, dc, e_row, e_col)


def solution(mesh):
    placed = (P("row", "col"), P(("row", "col"), None), P())
    return jax.shard_map(
        shards, mesh=mesh, in_specs=placed, out_specs=P("row", "col"), check_vma=False
    )
```

```python
import functools
import math

import jax
import jax.numpy as jnp
from jax import lax
from jax.experimental import pallas as pl
from jax.experimental.pallas import tpu as pltpu
from jax.sharding import PartitionSpec as P

ORDER = 16384
AUX = 768
COUPLING = ORDER / math.sqrt(AUX)
INV_ROOT = 1.0 / math.sqrt(ORDER)
MESH = pl.DeviceIdType.MESH
BF16, F32 = jnp.bfloat16, jnp.float32

SLOT = 128
HALF = SLOT // 2
K = AUX // 2
NT = (((1,), (1,)), ((), ()))
TN = (((0,), (0,)), ((), ()))


def part_of(ref, slot, k=None, offset=0, size=SLOT):
    rows = pl.ds(pl.multiple_of(slot * SLOT + offset, HALF), size)
    return ref.at[rows, :] if k is None else ref.at[rows, pl.ds(k * K, K)]


class Line:
    def __init__(self, device, slot, core=None):
        self.p, self.m, self.o, self.z = device(1, 0), device(3, 0), device(2, 0), device(0, 1)
        self.core = core
        self.own, self.own_z = slot(0, 0), slot(0, 1)
        self.sp, self.sp_z = slot(1, 0), slot(1, 1)
        self.sm, self.sm_z = slot(3, 0), slot(3, 1)
        self.so, self.so_z = slot(2, 0), slot(2, 1)


class Exchange:
    def __init__(self, send, recv):
        self.send, self.recv = send, recv
        self.started = []

    def copy(self, i, src, dst, target):
        return pltpu.make_async_remote_copy(
            src_ref=src, dst_ref=dst, send_sem=self.send.at[i], recv_sem=self.recv.at[i],
            device_id=target, device_id_type=MESH,
        )

    def go(self, i, src, dst, target):
        c = self.copy(i, src, dst, target)
        c.start()
        self.started.append(c)

    def got(self, i, dst, source):
        self.copy(i, dst, dst, source).wait_recv()

    def sent(self):
        for c in self.started:
            c.wait_send()
        self.started = []


class Gather(Exchange):
    def __init__(self, line, buf, k, send, recv, base=0, other=None, relay_own=False, relay_pair=False):
        super().__init__(send, recv)
        self.line, self.buf, self.k = line, buf, k
        self.base, self.other = base, other
        self.relay_own, self.relay_pair = relay_own, relay_pair

    def view(self, slot, offset=0, size=SLOT):
        return part_of(self.buf, self.base + slot, self.k, offset, size)

    def push(self, i, slot, target, offset=0, size=SLOT, src=None):
        dst = self.view(slot, offset, size)
        self.go(i, dst if src is None else src, dst, target)

    def arrived(self, i, slot, source, offset=0, size=SLOT):
        self.got(i, self.view(slot, offset, size), source)

    def to_core(self, i, slot):
        if self.other is not None:
            self.push(9 + i, slot, self.line.core)

    def start(self, src=None):
        ln = self.line
        self.push(2, ln.own, ln.z, src=src)
        if not self.relay_own:
            self.push(5, ln.own, ln.o, src=src)
        self.push(0, ln.own, ln.p, src=src)
        self.push(1, ln.own, ln.m, src=src)
        self.to_core(0, ln.own)

    def pair(self):
        ln = self.line
        self.arrived(2, ln.own_z, ln.z)
        if not self.relay_pair:
            self.push(7, ln.own_z, ln.o)
        self.push(3, ln.own_z, ln.p)
        self.push(4, ln.own_z, ln.m)
        self.to_core(1, ln.own_z)

    def near(self):
        ln = self.line
        self.arrived(0, ln.sm, ln.m)
        if self.relay_own:
            self.push(5, ln.sm, ln.p, 0, HALF)
        self.to_core(2, ln.sm)
        self.arrived(1, ln.sp, ln.p)
        if self.relay_own:
            self.push(6, ln.sp, ln.m, HALF, HALF)
        self.to_core(3, ln.sp)

    def near_pair(self):
        ln = self.line
        self.arrived(3, ln.sm_z, ln.m)
        if self.relay_pair:
            self.push(7, ln.sm_z, ln.p, 0, HALF)
        self.to_core(4, ln.sm_z)
        self.arrived(4, ln.sp_z, ln.p)
        if self.relay_pair:
            self.push(8, ln.sp_z, ln.m, HALF, HALF)
        self.to_core(5, ln.sp_z)

    def far(self):
        ln = self.line
        if self.relay_own:
            self.arrived(5, ln.so, ln.m, 0, HALF)
            self.arrived(6, ln.so, ln.p, HALF, HALF)
        else:
            self.arrived(5, ln.so, ln.o)
        self.to_core(6, ln.so)

    def far_pair(self):
        ln = self.line
        if self.relay_pair:
            self.arrived(7, ln.so_z, ln.m, 0, HALF)
            self.arrived(8, ln.so_z, ln.p, HALF, HALF)
        else:
            self.arrived(7, ln.so_z, ln.o)
        self.to_core(7, ln.so_z)

    def from_core(self, first=0, last=8):
        ln = self.line
        order = (ln.own, ln.own_z, ln.sm, ln.sp, ln.sm_z, ln.sp_z, ln.so, ln.so_z)
        for i in range(first, last):
            self.got(9 + i, part_of(self.buf, self.other + order[i], self.k), ln.core)


class Reduce(Exchange):
    def __init__(self, line, part, out, outz, into, inz, send, recv):
        super().__init__(send, recv)
        self.line, self.part = line, part
        self.out, self.outz, self.into, self.inz = out, outz, into, inz

    def give(self, d):
        ln = self.line
        slots, target = (
            ((ln.sp_z, ln.sp), ln.p), ((ln.sm_z, ln.sm), ln.m), ((ln.so_z, ln.so), ln.o),
        )[d]
        for h in range(2):
            self.out[d, h] = part_of(self.part, slots[h])[...].astype(BF16)
            self.go(2 * d + h, self.out.at[d, h], self.into.at[d, h], target)

    def collect(self, h):
        ln = self.line
        for d, source in ((0, ln.m), (1, ln.p), (2, ln.o)):
            self.got(2 * d + h, self.into.at[d, h], source)
        total = part_of(self.part, ln.own if h else ln.own_z)[...]
        for d in range(3):
            total = total + self.into[d, h].astype(F32)
        return total

    def pair(self):
        self.outz[...] = self.collect(0).astype(BF16)
        self.go(6, self.outz, self.inz, self.line.z)

    def total(self):
        total = self.collect(1)
        self.got(6, self.inz, self.line.z)
        return total + self.inz[...].astype(F32)


def spread_energies(energy, e_row, e_col):
    row, col = lax.axis_index("row"), lax.axis_index("col")
    for j in range(8):
        v = energy[pl.ds(row * 8 + j, 1), :]
        e_row[j * 128 : (j + 1) * 128, :] = jnp.broadcast_to(v, (128, 128)).T
    for j in range(16):
        e_col[:, j * 128 : (j + 1) * 128] = energy[pl.ds(col * 16 + j, 1), :]


def tile(dr, dc, e_row, e_col):
    residual = lax.dot_general(dr, dc, NT, preferred_element_type=F32)
    den = jnp.concatenate([e_row] * (residual.shape[1] // 128), axis=1) + e_col
    return -COUPLING * residual / den


def finish(dr, dc, e_row, e_col, out, stage, sem):
    def put(i):
        return pltpu.make_async_copy(stage.at[i % 2], out.at[pl.ds(i * 256, 256), :], sem.at[i % 2])

    for i in range(4):
        if i >= 2:
            put(i - 2).wait()
        for j in range(4):
            cols = slice(j * 512, (j + 1) * 512)
            rows = slice(i * 256, (i + 1) * 256)
            stage[i % 2, :, cols] = tile(dr[rows, :], dc[cols, :], e_row[rows, :], e_col[:, cols])
        put(i).start()
    put(2).wait()
    put(3).wait()


def cycle(
    amp, own_hbm, energy_hbm, dr1, dc1, e_row, e_col,
    a, stage, own, energy, fr, fc, own_c, dr0, dc0, part_r, part_c, core_out, core_in, weight,
    x_out, x_outz, x_in, x_inz, y_out, y_outz, y_in, y_inz,
    amp_sem, in_sem, turn_s, turn_r, agx_s, agx_r, agy_s, agy_r, rsx_s, rsx_r, rsy_s, rsy_r, co_s, co_r,
):
    row, col = lax.axis_index("row"), lax.axis_index("col")
    core, chip_row = lax.rem(row, 2), row // 2
    hi, y = chip_row // 4, lax.rem(chip_row, 4)
    x, lo = col // 2, lax.rem(col, 2)

    def at(r, c):
        return {"row": r, "col": c}

    def x_slot(step, flip):
        return lax.rem(x + step, 4) * 2 + (1 - lo if flip else lo)

    first_y = lax.rem(x, 2) * 2 + lo
    parity = x // 2 + lo

    def y_slot(step, flip):
        z = 1 - hi if flip else hi
        return lax.rem(x + y + step + 4 - first_y, 4) * 2 + lax.rem(z + parity, 2)

    def dev_x(step, flip):
        return at(row, x_slot(step, flip))

    def dev_y(step, flip):
        z = 1 - hi if flip else hi
        return at((z * 4 + lax.rem(y + step, 4)) * 2 + core, col)

    partner = at(chip_row * 2 + 1 - core, col)
    line_x = Line(dev_x, x_slot)
    line_y = Line(dev_y, y_slot, partner)

    x_to = chip_row // 2
    y_to = lax.rem(y + x + 4 - x_to, 4)
    hi_to = lax.rem(hi + lo + y, 2)
    to_row, to_col = (hi_to * 4 + y_to) * 2 + core, x_to * 2 + lax.rem(y, 2)
    turn_to = at(to_row, to_col)
    turn_from = at(col * 2 + core, line_y.own)
    moves = (to_row - row) * (to_row - row) + (to_col - col) * (to_col - col) != 0
    stays = jnp.logical_not(moves)

    half_c, other_c = core * 8, (1 - core) * 8
    mine_r, mine_c = line_x.own, half_c + line_y.own

    def turn(i, src, dst, device):
        return pltpu.make_async_remote_copy(
            src_ref=src, dst_ref=dst, send_sem=turn_s.at[i], recv_sem=turn_r.at[i],
            device_id=device, device_id_type=MESH,
        )

    def amp_copy(i):
        return pltpu.make_async_copy(amp.at[pl.ds(i * 256, 256), :], stage.at[i % 2], amp_sem.at[i % 2])

    own_copy = pltpu.make_async_copy(own_hbm, own, in_sem.at[0])
    energy_copy = pltpu.make_async_copy(energy_hbm, energy, in_sem.at[1])
    own_copy.start()
    energy_copy.start()
    amp_copy(0).start()
    amp_copy(1).start()

    barrier = pltpu.get_barrier_semaphore()

    def greet(device):
        pl.semaphore_signal(barrier, inc=1, device_id=device, device_id_type=MESH)

    for ln in (line_x, line_y):
        for device in (ln.p, ln.m, ln.o, ln.z):
            greet(device)
    greet(partner)

    @pl.when(moves)
    def _():
        greet(turn_to)
        greet(turn_from)

    own_copy.wait()

    @pl.when(moves)
    def _():
        pl.semaphore_wait(barrier, 11)

    @pl.when(stays)
    def _():
        pl.semaphore_wait(barrier, 9)

    gx = Gather(line_x, fr, None, agx_s.at[0], agx_r.at[0], relay_own=True, relay_pair=True)
    gy = Gather(line_y, fc, None, agy_s.at[0], agy_r.at[0], half_c, other_c, relay_own=True)
    own0, own1 = own.at[:, pl.ds(0, K)], own.at[:, pl.ds(K, K)]
    turn_f0 = turn(0, own0, part_of(fc, half_c + col), turn_to)
    turn_f1 = turn(1, own1, own_c, turn_to)

    @pl.when(moves)
    def _():
        turn_f0.start()

    gx.start(src=own1)

    @pl.when(moves)
    def _():
        turn_f1.start()

    part_of(fr, mine_r)[...] = own1[...]

    @pl.when(stays)
    def _():
        part_of(fc, mine_c)[...] = own0[...]
        own_c[...] = own1[...]

    energy_copy.wait()
    spread_energies(energy, e_row, e_col)
    for i in range(4):
        amp_copy(i).wait()
        a[i * 256 : (i + 1) * 256, :] = stage[i % 2].astype(BF16)
        if i + 2 < 4:
            amp_copy(i + 2).start()

    gx.pair()

    @pl.when(moves)
    def _():
        turn(0, own0, part_of(fc, mine_c), turn_from).wait_recv()

    gy.start()
    gx.near()
    gy.pair()
    gx.near_pair()
    gx.far()
    gy.near()
    gx.far_pair()

    def mm_rows(s):
        at_rows = pl.ds(pl.multiple_of((s // 2) * 256, 256), 256)
        part_r[at_rows, :] = jnp.dot(a[at_rows, :], fc[...], preferred_element_type=F32) * INV_ROOT

    def mm_cols(half, s, s_z):
        lhs = [a[:, pl.ds(pl.multiple_of((half + i) * SLOT, SLOT), SLOT)] for i in (s, s_z)]
        lhs = jnp.concatenate(lhs, axis=1)
        return lax.dot_general(lhs, fr[...], TN, preferred_element_type=F32) * INV_ROOT

    def new_tile(i, j):
        rows = pl.ds(pl.multiple_of(lax.rem(x + i, 4) * 256, 256), 256)
        first = lax.rem(x + y + j + 4 - first_y, 4) * 256
        cols = [pl.ds(pl.multiple_of(h * 1024 + first, 256), 256) for h in range(2)]
        residual = lax.dot_general(
            dr0[rows, :], jnp.concatenate([dc0[c, :] for c in cols], axis=0), NT, preferred_element_type=F32
        )
        for h in range(2):
            a[rows, cols[h]] = (residual[:, h * 256 : (h + 1) * 256] * weight[rows, cols[h]]).astype(BF16)

    def new_tiles(i):
        for j in (0, 1, 3):
            new_tile(i, j)

    pairs_y = (
        (line_y.so, line_y.so_z), (line_y.sp, line_y.sp_z), (line_y.sm, line_y.sm_z), (line_y.own, line_y.own_z),
    )

    for it in range(2):
        dr, dc = (dr0, dc0) if it == 0 else (dr1, dc1)
        rsx = Reduce(line_x, part_r, x_out, x_outz, x_in.at[it], x_inz.at[it], rsx_s.at[it], rsx_r.at[it])
        rsy = Reduce(line_y, part_c, y_out, y_outz, y_in.at[it], y_inz.at[it], rsy_s.at[it], rsy_r.at[it])

        def core_copy(i):
            return pltpu.make_async_remote_copy(
                src_ref=core_out.at[i], dst_ref=core_in.at[it, i],
                send_sem=co_s.at[it, i], recv_sem=co_r.at[it, i],
                device_id=partner, device_id_type=MESH,
            )

        def other_half(i):
            core_out[i] = mm_cols(other_c, *pairs_y[i]).astype(BF16)
            core_copy(i).start()

        def own_half(i):
            value = mm_cols(half_c, *pairs_y[i])
            core_copy(i).wait_recv()
            value = value + core_in[it, i].astype(F32)
            part_of(part_c, pairs_y[i][0])[...] = value[:SLOT]
            part_of(part_c, pairs_y[i][1])[...] = value[SLOT:]

        if it == 0:
            other_half(0)
            other_half(1)
            gy.near_pair()
            other_half(2)
            other_half(3)
            own_half(0)
            rsy.give(2)
            own_half(1)
            rsy.give(0)
            gy.far()
            gy.far_pair()
            own_half(2)
            rsy.give(1)
            own_half(3)
            gy.from_core()
            mm_rows(line_x.so)
            rsx.give(2)
            mm_rows(line_x.sp)
            rsx.give(0)
            mm_rows(line_x.sm)
            rsx.give(1)
            mm_rows(line_x.own)
        else:
            mm_rows(line_x.so)
            rsx.give(2)
            for i in (0, 1, 3):
                new_tile(i, 2)
            for i in range(4):
                other_half(i)
            own_half(0)
            rsy.give(2)
            mm_rows(line_x.sp)
            rsx.give(0)
            own_half(1)
            rsy.give(0)
            mm_rows(line_x.sm)
            rsx.give(1)
            own_half(2)
            rsy.give(1)
            own_half(3)
            mm_rows(line_x.own)
        rsy.pair()
        if it == 0:

            @pl.loop(0, 8)
            def _(i):
                rows = pl.ds(pl.multiple_of(i * 128, 128), 128)
                weight[rows, :] = -COUPLING / (jnp.concatenate([e_row[rows, :]] * 16, axis=1) + e_col[...])

        rsx.pair()

        hx = [
            Gather(
                line_x, dr, k, agx_s.at[1 + 2 * it + k], agx_r.at[1 + 2 * it + k],
                relay_own=True, relay_pair=k == 0,
            )
            for k in range(2)
        ]
        hy = [
            Gather(
                line_y, dc, k, agy_s.at[1 + 2 * it + k], agy_r.at[1 + 2 * it + k], half_c, other_c,
                relay_own=True, relay_pair=k == 1,
            )
            for k in range(2)
        ]
        r0, r1 = part_of(dr, mine_r, 0), part_of(dr, mine_r, 1)
        c0, c1 = part_of(dc, mine_c, 0), part_of(dc, mine_c, 1)
        turn_c = turn(2 + 2 * it, c1, part_of(dr, line_y.own, 1), turn_from)
        turn_r_ = turn(3 + 2 * it, r0, part_of(dc, half_c + col, 0), turn_to)

        if it == 0:

            @pl.when(moves)
            def _():
                turn(1, own1, own_c, turn_from).wait_recv()

        c1[...] = (own_c[...].astype(F32) + rsy.total()).astype(BF16)

        @pl.when(moves)
        def _():
            turn_c.start()

        hy[1].start()
        r0[...] = (own0[...].astype(F32) + rsx.total()).astype(BF16)

        @pl.when(moves)
        def _():
            turn_r_.start()

        hx[0].start()

        @pl.when(stays)
        def _():
            r1[...] = c1[...]
            c0[...] = r0[...]

        hy[1].pair()
        hx[0].pair()

        @pl.when(moves)
        def _():
            turn(2 + 2 * it, r1, r1, turn_to).wait_recv()

        hx[1].start()

        @pl.when(moves)
        def _():
            turn(3 + 2 * it, c0, c0, turn_from).wait_recv()

        hy[0].start()
        hy[1].near()
        hx[0].near()
        hy[1].near_pair()
        hx[0].near_pair()
        hy[0].pair()
        hx[1].pair()
        hy[1].far()
        hx[0].far()
        hy[0].near()
        hx[1].near()
        hy[1].far_pair()
        hx[0].far_pair()
        hy[0].near_pair()
        hx[1].near_pair()
        if it == 0:
            hy[1].from_core()
            hy[0].from_core(0, 6)
            new_tiles(0)
            hy[0].far()
            hx[1].far()
            new_tiles(1)
            hy[0].far_pair()
            hx[1].far_pair()
            new_tiles(3)
            hy[0].from_core(6, 8)
            for j in (0, 1, 3, 2):
                new_tile(2, j)
        else:
            hy[0].far()
            hx[1].far()
            hy[0].far_pair()
            hx[1].far_pair()
            hy[1].from_core()
            hy[0].from_core()

        for i in range(4):
            core_copy(i).wait_send()
        for exchange in (rsx, rsy, *hx, *hy):
            exchange.sent()

        @pl.when(moves)
        def _():
            turn_c.wait_send()
            turn_r_.wait_send()

    gx.sent()
    gy.sent()

    @pl.when(moves)
    def _():
        turn_f0.wait_send()
        turn_f1.wait_send()


def dma(*shape):
    return pltpu.SemaphoreType.DMA(shape)


def shards(amplitudes, factors, energies):
    row_tile, col_tile = amplitudes.shape
    vmem = pl.BlockSpec(memory_space=pltpu.VMEM)

    def line_buffers():
        return [
            pltpu.VMEM((3, 2, SLOT, K), BF16),
            pltpu.VMEM((SLOT, K), BF16),
            pltpu.VMEM((2, 3, 2, SLOT, K), BF16),
            pltpu.VMEM((2, SLOT, K), BF16),
        ]

    energy = energies.reshape(128, 128)
    hbm = pl.BlockSpec(memory_space=pltpu.MemorySpace.HBM)
    dr, dc, e_row, e_col = pl.pallas_call(
        cycle,
        out_shape=(
            jax.ShapeDtypeStruct((row_tile, AUX), BF16),
            jax.ShapeDtypeStruct((col_tile, AUX), BF16),
            jax.ShapeDtypeStruct((row_tile, 128), F32),
            jax.ShapeDtypeStruct((1, col_tile), F32),
        ),
        in_specs=[hbm, hbm, hbm],
        out_specs=(vmem, vmem, vmem, vmem),
        scratch_shapes=[
            pltpu.VMEM((row_tile, col_tile), BF16),
            pltpu.VMEM((2, 256, col_tile), F32),
            pltpu.VMEM((SLOT, AUX), BF16),
            pltpu.VMEM((128, 128), F32),
            pltpu.VMEM((row_tile, K), BF16),
            pltpu.VMEM((col_tile, K), BF16),
            pltpu.VMEM((SLOT, K), BF16),
            pltpu.VMEM((row_tile, AUX), BF16),
            pltpu.VMEM((col_tile, AUX), BF16),
            pltpu.VMEM((row_tile, K), F32),
            pltpu.VMEM((row_tile, K), F32),
            pltpu.VMEM((4, 256, K), BF16),
            pltpu.VMEM((2, 4, 256, K), BF16),
            pltpu.VMEM((row_tile, col_tile), F32),
            *line_buffers(),
            *line_buffers(),
            dma(2), dma(2), dma(6), dma(6),
            dma(5, 9), dma(5, 9), dma(5, 17), dma(5, 17),
            dma(2, 7), dma(2, 7), dma(2, 7), dma(2, 7),
            dma(2, 4), dma(2, 4),
        ],
        compiler_params=pltpu.CompilerParams(
            collective_id=0, has_side_effects=True, vmem_limit_bytes=46 * 1024 * 1024
        ),
        name="cycle",
    )(*(pltpu.with_memory_space_constraint(v, pltpu.MemorySpace.HBM) for v in (amplitudes, factors, energy)))

    return pl.pallas_call(
        finish,
        out_shape=jax.ShapeDtypeStruct((row_tile, col_tile), F32),
        in_specs=[vmem, vmem, vmem, vmem],
        out_specs=pl.BlockSpec(memory_space=pl.ANY),
        scratch_shapes=[pltpu.VMEM((2, 256, col_tile), F32), dma(2)],
        compiler_params=pltpu.CompilerParams(vmem_limit_bytes=20 * 1024 * 1024),
        name="finish",
    )(dr, dc, e_row, e_col)


def solution(mesh):
    placed = (P("row", "col"), P(("row", "col"), None), P())
    return jax.shard_map(
        shards, mesh=mesh, in_specs=placed, out_specs=P("row", "col"), check_vma=False
    )
```

```python
import functools
import math

import jax
import jax.numpy as jnp
from jax import lax
from jax.experimental import pallas as pl
from jax.experimental.pallas import tpu as pltpu
from jax.sharding import PartitionSpec as P

ORDER = 16384
AUX = 768
COUPLING = ORDER / math.sqrt(AUX)
INV_ROOT = 1.0 / math.sqrt(ORDER)
MESH = pl.DeviceIdType.MESH
BF16, F32 = jnp.bfloat16, jnp.float32

SLOT = 128
HALF = SLOT // 2
K = AUX // 2
NT = (((1,), (1,)), ((), ()))
TN = (((0,), (0,)), ((), ()))


def part_of(ref, slot, k=None, offset=0, size=SLOT):
    rows = pl.ds(pl.multiple_of(slot * SLOT + offset, HALF), size)
    return ref.at[rows, :] if k is None else ref.at[rows, pl.ds(k * K, K)]


class Line:
    def __init__(self, device, slot, core=None):
        self.p, self.m, self.o, self.z = device(1, 0), device(3, 0), device(2, 0), device(0, 1)
        self.core = core
        self.own, self.own_z = slot(0, 0), slot(0, 1)
        self.sp, self.sp_z = slot(1, 0), slot(1, 1)
        self.sm, self.sm_z = slot(3, 0), slot(3, 1)
        self.so, self.so_z = slot(2, 0), slot(2, 1)


class Exchange:
    def __init__(self, send, recv):
        self.send, self.recv = send, recv
        self.started = []

    def copy(self, i, src, dst, target):
        return pltpu.make_async_remote_copy(
            src_ref=src, dst_ref=dst, send_sem=self.send.at[i], recv_sem=self.recv.at[i],
            device_id=target, device_id_type=MESH,
        )

    def go(self, i, src, dst, target):
        c = self.copy(i, src, dst, target)
        c.start()
        self.started.append(c)

    def got(self, i, dst, source):
        self.copy(i, dst, dst, source).wait_recv()

    def sent(self):
        for c in self.started:
            c.wait_send()
        self.started = []


class Gather(Exchange):
    def __init__(self, line, buf, k, send, recv, base=0, other=None, relay_own=False, relay_pair=False):
        super().__init__(send, recv)
        self.line, self.buf, self.k = line, buf, k
        self.base, self.other = base, other
        self.relay_own, self.relay_pair = relay_own, relay_pair

    def view(self, slot, offset=0, size=SLOT):
        return part_of(self.buf, self.base + slot, self.k, offset, size)

    def push(self, i, slot, target, offset=0, size=SLOT, src=None):
        dst = self.view(slot, offset, size)
        self.go(i, dst if src is None else src, dst, target)

    def arrived(self, i, slot, source, offset=0, size=SLOT):
        self.got(i, self.view(slot, offset, size), source)

    def to_core(self, i, slot):
        if self.other is not None:
            self.push(9 + i, slot, self.line.core)

    def start(self, src=None):
        ln = self.line
        for h in range(2):
            half = None if src is None else src.at[pl.ds(h * HALF, HALF), :]
            self.push(17 * h + 2 * (1 - h), ln.own, ln.z, h * HALF, HALF, src=half)
        if not self.relay_own:
            self.push(5, ln.own, ln.o, src=src)
        self.push(0, ln.own, ln.p, src=src)
        self.push(1, ln.own, ln.m, src=src)
        self.to_core(0, ln.own)

    def pair(self):
        ln = self.line
        for h, (i, to_p, to_m) in enumerate(((2, 3, 4), (17, 18, 19))):
            self.arrived(i, ln.own_z, ln.z, h * HALF, HALF)
            if not self.relay_pair:
                self.push(7 + h, ln.own_z, ln.o, h * HALF, HALF)
            self.push(to_p, ln.own_z, ln.p, h * HALF, HALF)
            self.push(to_m, ln.own_z, ln.m, h * HALF, HALF)
        self.to_core(1, ln.own_z)

    def near(self):
        ln = self.line
        self.arrived(0, ln.sm, ln.m)
        if self.relay_own:
            self.push(5, ln.sm, ln.p, 0, HALF)
        self.to_core(2, ln.sm)
        self.arrived(1, ln.sp, ln.p)
        if self.relay_own:
            self.push(6, ln.sp, ln.m, HALF, HALF)
        self.to_core(3, ln.sp)

    def near_pair(self):
        ln = self.line
        self.arrived(3, ln.sm_z, ln.m, 0, HALF)
        if self.relay_pair:
            self.push(7, ln.sm_z, ln.p, 0, HALF)
        self.arrived(19, ln.sp_z, ln.p, HALF, HALF)
        if self.relay_pair:
            self.push(8, ln.sp_z, ln.m, HALF, HALF)
        self.arrived(18, ln.sm_z, ln.m, HALF, HALF)
        self.to_core(4, ln.sm_z)
        self.arrived(4, ln.sp_z, ln.p, 0, HALF)
        self.to_core(5, ln.sp_z)

    def far(self):
        ln = self.line
        if self.relay_own:
            self.arrived(5, ln.so, ln.m, 0, HALF)
            self.arrived(6, ln.so, ln.p, HALF, HALF)
        else:
            self.arrived(5, ln.so, ln.o)
        self.to_core(6, ln.so)

    def far_pair(self):
        ln = self.line
        if self.relay_pair:
            self.arrived(7, ln.so_z, ln.m, 0, HALF)
            self.arrived(8, ln.so_z, ln.p, HALF, HALF)
        else:
            self.arrived(7, ln.so_z, ln.o, 0, HALF)
            self.arrived(8, ln.so_z, ln.o, HALF, HALF)
        self.to_core(7, ln.so_z)

    def from_core(self, first=0, last=8):
        ln = self.line
        order = (ln.own, ln.own_z, ln.sm, ln.sp, ln.sm_z, ln.sp_z, ln.so, ln.so_z)
        for i in range(first, last):
            self.got(9 + i, part_of(self.buf, self.other + order[i], self.k), ln.core)


class Reduce(Exchange):
    def __init__(self, line, part, out, outz, into, inz, send, recv):
        super().__init__(send, recv)
        self.line, self.part = line, part
        self.out, self.outz, self.into, self.inz = out, outz, into, inz

    def give(self, d):
        ln = self.line
        slots, target = (
            ((ln.sp_z, ln.sp), ln.p), ((ln.sm_z, ln.sm), ln.m), ((ln.so_z, ln.so), ln.o),
        )[d]
        for h in range(2):
            self.out[d, h] = part_of(self.part, slots[h])[...].astype(BF16)
            self.go(2 * d + h, self.out.at[d, h], self.into.at[d, h], target)

    def collect(self, h):
        ln = self.line
        for d, source in ((0, ln.m), (1, ln.p), (2, ln.o)):
            self.got(2 * d + h, self.into.at[d, h], source)
        total = part_of(self.part, ln.own if h else ln.own_z)[...]
        for d in range(3):
            total = total + self.into[d, h].astype(F32)
        return total

    def pair(self):
        self.outz[...] = self.collect(0).astype(BF16)
        self.go(6, self.outz, self.inz, self.line.z)

    def total(self):
        total = self.collect(1)
        self.got(6, self.inz, self.line.z)
        return total + self.inz[...].astype(F32)


def spread_energies(energy, e_row, e_col):
    row, col = lax.axis_index("row"), lax.axis_index("col")
    for j in range(8):
        v = energy[pl.ds(row * 8 + j, 1), :]
        e_row[j * 128 : (j + 1) * 128, :] = jnp.broadcast_to(v, (128, 128)).T
    for j in range(16):
        e_col[:, j * 128 : (j + 1) * 128] = energy[pl.ds(col * 16 + j, 1), :]


def tile(dr, dc, e_row, e_col):
    residual = lax.dot_general(dr, dc, NT, preferred_element_type=F32)
    den = jnp.concatenate([e_row] * (residual.shape[1] // 128), axis=1) + e_col
    return -COUPLING * residual / den


def finish(dr, dc, e_row, e_col, out, stage, sem):
    def put(i):
        return pltpu.make_async_copy(stage.at[i % 2], out.at[pl.ds(i * 256, 256), :], sem.at[i % 2])

    for i in range(4):
        if i >= 2:
            put(i - 2).wait()
        for j in range(4):
            cols = slice(j * 512, (j + 1) * 512)
            rows = slice(i * 256, (i + 1) * 256)
            stage[i % 2, :, cols] = tile(dr[rows, :], dc[cols, :], e_row[rows, :], e_col[:, cols])
        put(i).start()
    put(2).wait()
    put(3).wait()


def cycle(
    amp, own_hbm, energy_hbm, dr1, dc1, e_row, e_col,
    a, stage, own, energy, fr, fc, own_c, dr0, dc0, part_r, part_c, core_out, core_in, weight,
    x_out, x_outz, x_in, x_inz, y_out, y_outz, y_in, y_inz,
    amp_sem, in_sem, turn_s, turn_r, agx_s, agx_r, agy_s, agy_r, rsx_s, rsx_r, rsy_s, rsy_r, co_s, co_r,
):
    row, col = lax.axis_index("row"), lax.axis_index("col")
    core, chip_row = lax.rem(row, 2), row // 2
    hi, y = chip_row // 4, lax.rem(chip_row, 4)
    x, lo = col // 2, lax.rem(col, 2)

    def at(r, c):
        return {"row": r, "col": c}

    def x_slot(step, flip):
        return lax.rem(x + step, 4) * 2 + (1 - lo if flip else lo)

    first_y = lax.rem(x, 2) * 2 + lo
    parity = x // 2 + lo

    def y_slot(step, flip):
        z = 1 - hi if flip else hi
        return lax.rem(x + y + step + 4 - first_y, 4) * 2 + lax.rem(z + parity, 2)

    def dev_x(step, flip):
        return at(row, x_slot(step, flip))

    def dev_y(step, flip):
        z = 1 - hi if flip else hi
        return at((z * 4 + lax.rem(y + step, 4)) * 2 + core, col)

    partner = at(chip_row * 2 + 1 - core, col)
    line_x = Line(dev_x, x_slot)
    line_y = Line(dev_y, y_slot, partner)

    x_to = chip_row // 2
    y_to = lax.rem(y + x + 4 - x_to, 4)
    hi_to = lax.rem(hi + lo + y, 2)
    to_row, to_col = (hi_to * 4 + y_to) * 2 + core, x_to * 2 + lax.rem(y, 2)
    turn_to = at(to_row, to_col)
    turn_from = at(col * 2 + core, line_y.own)
    moves = (to_row - row) * (to_row - row) + (to_col - col) * (to_col - col) != 0
    stays = jnp.logical_not(moves)

    half_c, other_c = core * 8, (1 - core) * 8
    mine_r, mine_c = line_x.own, half_c + line_y.own

    def turn(i, src, dst, device):
        return pltpu.make_async_remote_copy(
            src_ref=src, dst_ref=dst, send_sem=turn_s.at[i], recv_sem=turn_r.at[i],
            device_id=device, device_id_type=MESH,
        )

    def amp_copy(i):
        return pltpu.make_async_copy(amp.at[pl.ds(i * 256, 256), :], stage.at[i % 2], amp_sem.at[i % 2])

    own_copy = pltpu.make_async_copy(own_hbm, own, in_sem.at[0])
    energy_copy = pltpu.make_async_copy(energy_hbm, energy, in_sem.at[1])
    own_copy.start()
    energy_copy.start()
    amp_copy(0).start()
    amp_copy(1).start()

    barrier = pltpu.get_barrier_semaphore()

    def greet(device):
        pl.semaphore_signal(barrier, inc=1, device_id=device, device_id_type=MESH)

    for ln in (line_x, line_y):
        for device in (ln.p, ln.m, ln.o, ln.z):
            greet(device)
    greet(partner)

    @pl.when(moves)
    def _():
        greet(turn_to)
        greet(turn_from)

    def take_amp(i):
        amp_copy(i).wait()
        a[i * 256 : (i + 1) * 256, :] = stage[i % 2].astype(BF16)
        if i + 2 < 4:
            amp_copy(i + 2).start()

    own_copy.wait()
    take_amp(0)

    @pl.when(moves)
    def _():
        pl.semaphore_wait(barrier, 11)

    @pl.when(stays)
    def _():
        pl.semaphore_wait(barrier, 9)

    gx = Gather(line_x, fr, None, agx_s.at[0], agx_r.at[0], relay_own=True, relay_pair=True)
    gy = Gather(line_y, fc, None, agy_s.at[0], agy_r.at[0], half_c, other_c, relay_own=True)
    own0, own1 = own.at[:, pl.ds(0, K)], own.at[:, pl.ds(K, K)]
    turn_f0 = turn(0, own0, part_of(fc, half_c + col), turn_to)
    turn_f1 = turn(1, own1, own_c, turn_to)

    @pl.when(moves)
    def _():
        turn_f0.start()

    gx.start(src=own1)
    part_of(fr, mine_r)[...] = own1[...]

    @pl.when(stays)
    def _():
        part_of(fc, mine_c)[...] = own0[...]
        own_c[...] = own1[...]

    take_amp(1)
    take_amp(2)
    gx.pair()
    take_amp(3)
    energy_copy.wait()
    spread_energies(energy, e_row, e_col)

    @pl.when(moves)
    def _():
        turn(0, own0, part_of(fc, mine_c), turn_from).wait_recv()

    gy.start()
    gx.near()
    gy.pair()
    gx.near_pair()
    gx.far()
    gy.near()
    gx.far_pair()

    @pl.when(moves)
    def _():
        turn_f1.start()


    def mm_rows(s):
        at_rows = pl.ds(pl.multiple_of((s // 2) * 256, 256), 256)
        part_r[at_rows, :] = jnp.dot(a[at_rows, :], fc[...], preferred_element_type=F32) * INV_ROOT

    def mm_cols(half, s, s_z):
        lhs = [a[:, pl.ds(pl.multiple_of((half + i) * SLOT, SLOT), SLOT)] for i in (s, s_z)]
        lhs = jnp.concatenate(lhs, axis=1)
        return lax.dot_general(lhs, fr[...], TN, preferred_element_type=F32) * INV_ROOT

    def new_tile(i, j):
        rows = pl.ds(pl.multiple_of(lax.rem(x + i, 4) * 256, 256), 256)
        first = lax.rem(x + y + j + 4 - first_y, 4) * 256
        cols = [pl.ds(pl.multiple_of(h * 1024 + first, 256), 256) for h in range(2)]
        residual = lax.dot_general(
            dr0[rows, :], jnp.concatenate([dc0[c, :] for c in cols], axis=0), NT, preferred_element_type=F32
        )
        for h in range(2):
            a[rows, cols[h]] = (residual[:, h * 256 : (h + 1) * 256] * weight[rows, cols[h]]).astype(BF16)

    def new_tiles(i):
        for j in (0, 1, 3):
            new_tile(i, j)

    pairs_y = (
        (line_y.so, line_y.so_z), (line_y.sp, line_y.sp_z), (line_y.sm, line_y.sm_z), (line_y.own, line_y.own_z),
    )

    for it in range(2):
        dr, dc = (dr0, dc0) if it == 0 else (dr1, dc1)
        rsx = Reduce(line_x, part_r, x_out, x_outz, x_in.at[it], x_inz.at[it], rsx_s.at[it], rsx_r.at[it])
        rsy = Reduce(line_y, part_c, y_out, y_outz, y_in.at[it], y_inz.at[it], rsy_s.at[it], rsy_r.at[it])

        def core_copy(i):
            return pltpu.make_async_remote_copy(
                src_ref=core_out.at[i], dst_ref=core_in.at[it, i],
                send_sem=co_s.at[it, i], recv_sem=co_r.at[it, i],
                device_id=partner, device_id_type=MESH,
            )

        def other_half(i):
            core_out[i] = mm_cols(other_c, *pairs_y[i]).astype(BF16)
            core_copy(i).start()

        def own_half(i):
            value = mm_cols(half_c, *pairs_y[i])
            core_copy(i).wait_recv()
            value = value + core_in[it, i].astype(F32)
            part_of(part_c, pairs_y[i][0])[...] = value[:SLOT]
            part_of(part_c, pairs_y[i][1])[...] = value[SLOT:]

        if it == 0:
            other_half(0)
            other_half(1)
            gy.near_pair()
            other_half(2)
            other_half(3)
            own_half(0)
            rsy.give(2)
            own_half(1)
            rsy.give(0)
            gy.far()
            gy.far_pair()
            own_half(2)
            rsy.give(1)
            own_half(3)
            gy.from_core()
            mm_rows(line_x.so)
            rsx.give(2)
            mm_rows(line_x.sp)
            rsx.give(0)
            mm_rows(line_x.sm)
            rsx.give(1)
            mm_rows(line_x.own)
        else:
            mm_rows(line_x.so)
            rsx.give(2)
            for i in (0, 1, 3):
                new_tile(i, 2)
            other_half(0)
            other_half(1)
            own_half(0)
            rsy.give(2)
            other_half(2)
            own_half(1)
            rsy.give(0)
            mm_rows(line_x.sp)
            rsx.give(0)
            other_half(3)
            own_half(2)
            rsy.give(1)
            mm_rows(line_x.sm)
            rsx.give(1)
            own_half(3)
            mm_rows(line_x.own)
        rsy.pair()
        if it == 0:

            @pl.loop(0, 8)
            def _(i):
                rows = pl.ds(pl.multiple_of(i * 128, 128), 128)
                weight[rows, :] = -COUPLING / (jnp.concatenate([e_row[rows, :]] * 16, axis=1) + e_col[...])

        rsx.pair()

        hx = [
            Gather(
                line_x, dr, k, agx_s.at[1 + 2 * it + k], agx_r.at[1 + 2 * it + k],
                relay_own=True, relay_pair=k == 0,
            )
            for k in range(2)
        ]
        hy = [
            Gather(
                line_y, dc, k, agy_s.at[1 + 2 * it + k], agy_r.at[1 + 2 * it + k], half_c, other_c,
                relay_own=True, relay_pair=k == 1,
            )
            for k in range(2)
        ]
        r0, r1 = part_of(dr, mine_r, 0), part_of(dr, mine_r, 1)
        c0, c1 = part_of(dc, mine_c, 0), part_of(dc, mine_c, 1)
        turn_c = turn(2 + 2 * it, c1, part_of(dr, line_y.own, 1), turn_from)
        turn_r_ = turn(3 + 2 * it, r0, part_of(dc, half_c + col, 0), turn_to)

        if it == 0:

            @pl.when(moves)
            def _():
                turn(1, own1, own_c, turn_from).wait_recv()

        c1[...] = (own_c[...].astype(F32) + rsy.total()).astype(BF16)

        @pl.when(moves)
        def _():
            turn_c.start()

        hy[1].start()
        r0[...] = (own0[...].astype(F32) + rsx.total()).astype(BF16)

        @pl.when(moves)
        def _():
            turn_r_.start()

        hx[0].start()

        @pl.when(stays)
        def _():
            r1[...] = c1[...]
            c0[...] = r0[...]

        hy[1].pair()
        hx[0].pair()

        @pl.when(moves)
        def _():
            turn(2 + 2 * it, r1, r1, turn_to).wait_recv()

        hx[1].start()

        @pl.when(moves)
        def _():
            turn(3 + 2 * it, c0, c0, turn_from).wait_recv()

        hy[0].start()
        hy[1].near()
        hx[0].near()
        hy[1].near_pair()
        hx[0].near_pair()
        hy[0].pair()
        hx[1].pair()
        hy[1].far()
        hx[0].far()
        hy[0].near()
        hx[1].near()
        hy[1].far_pair()
        hx[0].far_pair()
        hy[0].near_pair()
        hx[1].near_pair()
        if it == 0:
            hy[1].from_core()
            hy[0].from_core(0, 6)
            new_tiles(0)
            hy[0].far()
            hx[1].far()
            new_tiles(1)
            hy[0].far_pair()
            hx[1].far_pair()
            new_tiles(3)
            hy[0].from_core(6, 8)
            for j in (0, 1, 3, 2):
                new_tile(2, j)
        else:
            hy[0].far()
            hx[1].far()
            hy[0].far_pair()
            hx[1].far_pair()
            hy[1].from_core()
            hy[0].from_core()

        for i in range(4):
            core_copy(i).wait_send()
        for exchange in (rsx, rsy, *hx, *hy):
            exchange.sent()

        @pl.when(moves)
        def _():
            turn_c.wait_send()
            turn_r_.wait_send()

    gx.sent()
    gy.sent()

    @pl.when(moves)
    def _():
        turn_f0.wait_send()
        turn_f1.wait_send()


def dma(*shape):
    return pltpu.SemaphoreType.DMA(shape)


def shards(amplitudes, factors, energies):
    row_tile, col_tile = amplitudes.shape
    vmem = pl.BlockSpec(memory_space=pltpu.VMEM)

    def line_buffers():
        return [
            pltpu.VMEM((3, 2, SLOT, K), BF16),
            pltpu.VMEM((SLOT, K), BF16),
            pltpu.VMEM((2, 3, 2, SLOT, K), BF16),
            pltpu.VMEM((2, SLOT, K), BF16),
        ]

    energy = energies.reshape(128, 128)
    hbm = pl.BlockSpec(memory_space=pltpu.MemorySpace.HBM)
    dr, dc, e_row, e_col = pl.pallas_call(
        cycle,
        out_shape=(
            jax.ShapeDtypeStruct((row_tile, AUX), BF16),
            jax.ShapeDtypeStruct((col_tile, AUX), BF16),
            jax.ShapeDtypeStruct((row_tile, 128), F32),
            jax.ShapeDtypeStruct((1, col_tile), F32),
        ),
        in_specs=[hbm, hbm, hbm],
        out_specs=(vmem, vmem, vmem, vmem),
        scratch_shapes=[
            pltpu.VMEM((row_tile, col_tile), BF16),
            pltpu.VMEM((2, 256, col_tile), F32),
            pltpu.VMEM((SLOT, AUX), BF16),
            pltpu.VMEM((128, 128), F32),
            pltpu.VMEM((row_tile, K), BF16),
            pltpu.VMEM((col_tile, K), BF16),
            pltpu.VMEM((SLOT, K), BF16),
            pltpu.VMEM((row_tile, AUX), BF16),
            pltpu.VMEM((col_tile, AUX), BF16),
            pltpu.VMEM((row_tile, K), F32),
            pltpu.VMEM((row_tile, K), F32),
            pltpu.VMEM((4, 256, K), BF16),
            pltpu.VMEM((2, 4, 256, K), BF16),
            pltpu.VMEM((row_tile, col_tile), F32),
            *line_buffers(),
            *line_buffers(),
            dma(2), dma(2), dma(6), dma(6),
            dma(5, 20), dma(5, 20), dma(5, 20), dma(5, 20),
            dma(2, 7), dma(2, 7), dma(2, 7), dma(2, 7),
            dma(2, 4), dma(2, 4),
        ],
        compiler_params=pltpu.CompilerParams(
            collective_id=0, has_side_effects=True, vmem_limit_bytes=46 * 1024 * 1024
        ),
        name="cycle",
    )(*(pltpu.with_memory_space_constraint(v, pltpu.MemorySpace.HBM) for v in (amplitudes, factors, energy)))

    return pl.pallas_call(
        finish,
        out_shape=jax.ShapeDtypeStruct((row_tile, col_tile), F32),
        in_specs=[vmem, vmem, vmem, vmem],
        out_specs=pl.BlockSpec(memory_space=pl.ANY),
        scratch_shapes=[pltpu.VMEM((2, 256, col_tile), F32), dma(2)],
        compiler_params=pltpu.CompilerParams(vmem_limit_bytes=20 * 1024 * 1024),
        name="finish",
    )(dr, dc, e_row, e_col)


def solution(mesh):
    placed = (P("row", "col"), P(("row", "col"), None), P())
    return jax.shard_map(
        shards, mesh=mesh, in_specs=placed, out_specs=P("row", "col"), check_vma=False
    )
```

```python
import functools
import math

import jax
import jax.numpy as jnp
from jax import lax
from jax.experimental import pallas as pl
from jax.experimental.pallas import tpu as pltpu
from jax.sharding import PartitionSpec as P

ORDER = 16384
AUX = 768
COUPLING = ORDER / math.sqrt(AUX)
INV_ROOT = 1.0 / math.sqrt(ORDER)
MESH = pl.DeviceIdType.MESH
BF16, F32 = jnp.bfloat16, jnp.float32

SLOT = 128
HALF = SLOT // 2
K = AUX // 2
NT = (((1,), (1,)), ((), ()))
TN = (((0,), (0,)), ((), ()))


def part_of(ref, slot, k=None, offset=0, size=SLOT):
    rows = pl.ds(pl.multiple_of(slot * SLOT + offset, HALF), size)
    return ref.at[rows, :] if k is None else ref.at[rows, pl.ds(k * K, K)]


class Line:
    def __init__(self, device, slot, core=None):
        self.p, self.m, self.o, self.z = device(1, 0), device(3, 0), device(2, 0), device(0, 1)
        self.core = core
        self.own, self.own_z = slot(0, 0), slot(0, 1)
        self.sp, self.sp_z = slot(1, 0), slot(1, 1)
        self.sm, self.sm_z = slot(3, 0), slot(3, 1)
        self.so, self.so_z = slot(2, 0), slot(2, 1)


class Exchange:
    def __init__(self, send, recv):
        self.send, self.recv = send, recv
        self.started = []

    def copy(self, i, src, dst, target):
        return pltpu.make_async_remote_copy(
            src_ref=src, dst_ref=dst, send_sem=self.send.at[i], recv_sem=self.recv.at[i],
            device_id=target, device_id_type=MESH,
        )

    def go(self, i, src, dst, target):
        c = self.copy(i, src, dst, target)
        c.start()
        self.started.append(c)

    def got(self, i, dst, source):
        self.copy(i, dst, dst, source).wait_recv()

    def sent(self):
        for c in self.started:
            c.wait_send()
        self.started = []


class Gather(Exchange):
    def __init__(self, line, buf, k, send, recv, base=0, other=None, relay_own=False, relay_pair=False):
        super().__init__(send, recv)
        self.line, self.buf, self.k = line, buf, k
        self.base, self.other = base, other
        self.relay_own, self.relay_pair = relay_own, relay_pair

    def view(self, slot, offset=0, size=SLOT):
        return part_of(self.buf, self.base + slot, self.k, offset, size)

    def push(self, i, slot, target, offset=0, size=SLOT, src=None):
        dst = self.view(slot, offset, size)
        self.go(i, dst if src is None else src, dst, target)

    def arrived(self, i, slot, source, offset=0, size=SLOT):
        self.got(i, self.view(slot, offset, size), source)

    def to_core(self, i, slot):
        if self.other is not None:
            self.push(9 + i, slot, self.line.core)

    def start(self, src=None):
        ln = self.line
        for h in range(2):
            half = None if src is None else src.at[pl.ds(h * HALF, HALF), :]
            self.push(17 * h + 2 * (1 - h), ln.own, ln.z, h * HALF, HALF, src=half)
        if not self.relay_own:
            self.push(5, ln.own, ln.o, src=src)
        self.push(0, ln.own, ln.p, src=src)
        self.push(1, ln.own, ln.m, src=src)
        self.to_core(0, ln.own)

    def pair(self):
        ln = self.line
        for h, (i, to_p, to_m) in enumerate(((2, 3, 4), (17, 18, 19))):
            self.arrived(i, ln.own_z, ln.z, h * HALF, HALF)
            if not self.relay_pair:
                self.push(7 + h, ln.own_z, ln.o, h * HALF, HALF)
            self.push(to_p, ln.own_z, ln.p, h * HALF, HALF)
            self.push(to_m, ln.own_z, ln.m, h * HALF, HALF)
        self.to_core(1, ln.own_z)

    def near(self):
        ln = self.line
        self.arrived(0, ln.sm, ln.m)
        if self.relay_own:
            self.push(5, ln.sm, ln.p, 0, HALF)
        self.to_core(2, ln.sm)
        self.arrived(1, ln.sp, ln.p)
        if self.relay_own:
            self.push(6, ln.sp, ln.m, HALF, HALF)
        self.to_core(3, ln.sp)

    def near_pair(self):
        ln = self.line
        self.arrived(3, ln.sm_z, ln.m, 0, HALF)
        if self.relay_pair:
            self.push(7, ln.sm_z, ln.p, 0, HALF)
        self.arrived(19, ln.sp_z, ln.p, HALF, HALF)
        if self.relay_pair:
            self.push(8, ln.sp_z, ln.m, HALF, HALF)
        self.arrived(18, ln.sm_z, ln.m, HALF, HALF)
        self.to_core(4, ln.sm_z)
        self.arrived(4, ln.sp_z, ln.p, 0, HALF)
        self.to_core(5, ln.sp_z)

    def far(self):
        ln = self.line
        if self.relay_own:
            self.arrived(5, ln.so, ln.m, 0, HALF)
            self.arrived(6, ln.so, ln.p, HALF, HALF)
        else:
            self.arrived(5, ln.so, ln.o)
        self.to_core(6, ln.so)

    def far_pair(self):
        ln = self.line
        if self.relay_pair:
            self.arrived(7, ln.so_z, ln.m, 0, HALF)
            self.arrived(8, ln.so_z, ln.p, HALF, HALF)
        else:
            self.arrived(7, ln.so_z, ln.o, 0, HALF)
            self.arrived(8, ln.so_z, ln.o, HALF, HALF)
        self.to_core(7, ln.so_z)

    def from_core(self, first=0, last=8):
        ln = self.line
        order = (ln.own, ln.own_z, ln.sm, ln.sp, ln.sm_z, ln.sp_z, ln.so, ln.so_z)
        for i in range(first, last):
            self.got(9 + i, part_of(self.buf, self.other + order[i], self.k), ln.core)


class Reduce(Exchange):
    def __init__(self, line, part, out, outz, into, inz, send, recv):
        super().__init__(send, recv)
        self.line, self.part = line, part
        self.out, self.outz, self.into, self.inz = out, outz, into, inz

    def give(self, d):
        ln = self.line
        slots, target = (
            ((ln.sp_z, ln.sp), ln.p), ((ln.sm_z, ln.sm), ln.m), ((ln.so_z, ln.so), ln.o),
        )[d]
        for h in range(2):
            self.out[d, h] = part_of(self.part, slots[h])[...].astype(BF16)
            self.go(2 * d + h, self.out.at[d, h], self.into.at[d, h], target)

    def collect(self, h):
        ln = self.line
        for d, source in ((0, ln.m), (1, ln.p), (2, ln.o)):
            self.got(2 * d + h, self.into.at[d, h], source)
        total = part_of(self.part, ln.own if h else ln.own_z)[...]
        for d in range(3):
            total = total + self.into[d, h].astype(F32)
        return total

    def pair(self):
        self.outz[...] = self.collect(0).astype(BF16)
        self.go(6, self.outz, self.inz, self.line.z)

    def total(self):
        total = self.collect(1)
        self.got(6, self.inz, self.line.z)
        return total + self.inz[...].astype(F32)


def spread_energies(energy, e_row, e_col):
    row, col = lax.axis_index("row"), lax.axis_index("col")
    for j in range(8):
        v = energy[pl.ds(row * 8 + j, 1), :]
        e_row[j * 128 : (j + 1) * 128, :] = jnp.broadcast_to(v, (128, 128)).T
    for j in range(16):
        e_col[:, j * 128 : (j + 1) * 128] = energy[pl.ds(col * 16 + j, 1), :]


def tile(dr, dc, e_row, e_col):
    residual = lax.dot_general(dr, dc, NT, preferred_element_type=F32)
    den = jnp.concatenate([e_row] * (residual.shape[1] // 128), axis=1) + e_col
    return -COUPLING * residual / den


def finish(dr, dc, e_row, e_col, out, stage, sem):
    def put(i, j):
        part = out.at[pl.ds(i * 256, 256), pl.ds(j * 512, 512)]
        return pltpu.make_async_copy(stage.at[i % 2, j], part, sem.at[i % 2, j])

    for i in range(4):
        rows = slice(i * 256, (i + 1) * 256)
        for j in range(4):
            cols = slice(j * 512, (j + 1) * 512)
            if i >= 2:
                put(i - 2, j).wait()
            stage[i % 2, j] = tile(dr[rows, :], dc[cols, :], e_row[rows, :], e_col[:, cols])
            put(i, j).start()
    for i in (2, 3):
        for j in range(4):
            put(i, j).wait()


def cycle(
    amp, own_hbm, energy_hbm, dr1, dc1, e_row, e_col,
    a, stage, own, energy, fr, fc, own_c, dr0, dc0, part_r, part_c, core_out, core_in, weight,
    x_out, x_outz, x_in, x_inz, y_out, y_outz, y_in, y_inz,
    amp_sem, in_sem, turn_s, turn_r, agx_s, agx_r, agy_s, agy_r, rsx_s, rsx_r, rsy_s, rsy_r, co_s, co_r,
):
    row, col = lax.axis_index("row"), lax.axis_index("col")
    core, chip_row = lax.rem(row, 2), row // 2
    hi, y = chip_row // 4, lax.rem(chip_row, 4)
    x, lo = col // 2, lax.rem(col, 2)

    def at(r, c):
        return {"row": r, "col": c}

    def x_slot(step, flip):
        return lax.rem(x + step, 4) * 2 + (1 - lo if flip else lo)

    first_y = lax.rem(x, 2) * 2 + lo
    parity = x // 2 + lo

    def y_slot(step, flip):
        z = 1 - hi if flip else hi
        return lax.rem(x + y + step + 4 - first_y, 4) * 2 + lax.rem(z + parity, 2)

    def dev_x(step, flip):
        return at(row, x_slot(step, flip))

    def dev_y(step, flip):
        z = 1 - hi if flip else hi
        return at((z * 4 + lax.rem(y + step, 4)) * 2 + core, col)

    partner = at(chip_row * 2 + 1 - core, col)
    line_x = Line(dev_x, x_slot)
    line_y = Line(dev_y, y_slot, partner)

    x_to = chip_row // 2
    y_to = lax.rem(y + x + 4 - x_to, 4)
    hi_to = lax.rem(hi + lo + y, 2)
    to_row, to_col = (hi_to * 4 + y_to) * 2 + core, x_to * 2 + lax.rem(y, 2)
    turn_to = at(to_row, to_col)
    turn_from = at(col * 2 + core, line_y.own)
    moves = (to_row - row) * (to_row - row) + (to_col - col) * (to_col - col) != 0
    stays = jnp.logical_not(moves)

    half_c, other_c = core * 8, (1 - core) * 8
    mine_r, mine_c = line_x.own, half_c + line_y.own

    def turn(i, src, dst, device):
        return pltpu.make_async_remote_copy(
            src_ref=src, dst_ref=dst, send_sem=turn_s.at[i], recv_sem=turn_r.at[i],
            device_id=device, device_id_type=MESH,
        )

    def amp_copy(i):
        return pltpu.make_async_copy(amp.at[pl.ds(i * 256, 256), :], stage.at[i % 2], amp_sem.at[i % 2])

    own_copy = pltpu.make_async_copy(own_hbm, own, in_sem.at[0])
    energy_copy = pltpu.make_async_copy(energy_hbm, energy, in_sem.at[1])
    own_copy.start()
    energy_copy.start()
    amp_copy(0).start()
    amp_copy(1).start()

    barrier = pltpu.get_barrier_semaphore()

    def greet(device):
        pl.semaphore_signal(barrier, inc=1, device_id=device, device_id_type=MESH)

    for ln in (line_x, line_y):
        for device in (ln.p, ln.m, ln.o, ln.z):
            greet(device)
    greet(partner)

    @pl.when(moves)
    def _():
        greet(turn_to)
        greet(turn_from)

    def take_amp(i):
        amp_copy(i).wait()
        a[i * 256 : (i + 1) * 256, :] = stage[i % 2].astype(BF16)
        if i + 2 < 4:
            amp_copy(i + 2).start()

    own_copy.wait()
    take_amp(0)

    @pl.when(moves)
    def _():
        pl.semaphore_wait(barrier, 11)

    @pl.when(stays)
    def _():
        pl.semaphore_wait(barrier, 9)

    gx = Gather(line_x, fr, None, agx_s.at[0], agx_r.at[0], relay_own=True, relay_pair=True)
    gy = Gather(line_y, fc, None, agy_s.at[0], agy_r.at[0], half_c, other_c, relay_own=True)
    own0, own1 = own.at[:, pl.ds(0, K)], own.at[:, pl.ds(K, K)]
    turn_f0 = turn(0, own0, part_of(fc, half_c + col), turn_to)
    turn_f1 = turn(1, own1, own_c, turn_to)

    @pl.when(moves)
    def _():
        turn_f0.start()

    gx.start(src=own1)
    part_of(fr, mine_r)[...] = own1[...]

    @pl.when(stays)
    def _():
        part_of(fc, mine_c)[...] = own0[...]
        own_c[...] = own1[...]

    take_amp(1)
    take_amp(2)
    gx.pair()
    take_amp(3)
    energy_copy.wait()
    spread_energies(energy, e_row, e_col)

    @pl.when(moves)
    def _():
        turn(0, own0, part_of(fc, mine_c), turn_from).wait_recv()

    gy.start()
    gx.near()
    gy.pair()
    gx.near_pair()
    gx.far()
    gy.near()
    gx.far_pair()

    @pl.when(moves)
    def _():
        turn_f1.start()


    def mm_rows(s):
        at_rows = pl.ds(pl.multiple_of((s // 2) * 256, 256), 256)
        part_r[at_rows, :] = jnp.dot(a[at_rows, :], fc[...], preferred_element_type=F32) * INV_ROOT

    def mm_cols(half, s, s_z):
        lhs = [a[:, pl.ds(pl.multiple_of((half + i) * SLOT, SLOT), SLOT)] for i in (s, s_z)]
        lhs = jnp.concatenate(lhs, axis=1)
        return lax.dot_general(lhs, fr[...], TN, preferred_element_type=F32) * INV_ROOT

    def new_tile(i, j):
        rows = pl.ds(pl.multiple_of(lax.rem(x + i, 4) * 256, 256), 256)
        first = lax.rem(x + y + j + 4 - first_y, 4) * 256
        cols = [pl.ds(pl.multiple_of(h * 1024 + first, 256), 256) for h in range(2)]
        residual = lax.dot_general(
            dr0[rows, :], jnp.concatenate([dc0[c, :] for c in cols], axis=0), NT, preferred_element_type=F32
        )
        for h in range(2):
            a[rows, cols[h]] = (residual[:, h * 256 : (h + 1) * 256] * weight[rows, cols[h]]).astype(BF16)

    def new_tiles(i):
        for j in (0, 1, 3):
            new_tile(i, j)

    pairs_y = (
        (line_y.so, line_y.so_z), (line_y.sp, line_y.sp_z), (line_y.sm, line_y.sm_z), (line_y.own, line_y.own_z),
    )

    for it in range(2):
        dr, dc = (dr0, dc0) if it == 0 else (dr1, dc1)
        rsx = Reduce(line_x, part_r, x_out, x_outz, x_in.at[it], x_inz.at[it], rsx_s.at[it], rsx_r.at[it])
        rsy = Reduce(line_y, part_c, y_out, y_outz, y_in.at[it], y_inz.at[it], rsy_s.at[it], rsy_r.at[it])

        def core_copy(i):
            return pltpu.make_async_remote_copy(
                src_ref=core_out.at[i], dst_ref=core_in.at[it, i],
                send_sem=co_s.at[it, i], recv_sem=co_r.at[it, i],
                device_id=partner, device_id_type=MESH,
            )

        def other_half(i):
            core_out[i] = mm_cols(other_c, *pairs_y[i]).astype(BF16)
            core_copy(i).start()

        def own_half(i):
            value = mm_cols(half_c, *pairs_y[i])
            core_copy(i).wait_recv()
            value = value + core_in[it, i].astype(F32)
            part_of(part_c, pairs_y[i][0])[...] = value[:SLOT]
            part_of(part_c, pairs_y[i][1])[...] = value[SLOT:]

        if it == 0:
            other_half(0)
            other_half(1)
            gy.near_pair()
            other_half(2)
            other_half(3)
            own_half(0)
            rsy.give(2)
            own_half(1)
            rsy.give(0)
            gy.far()
            gy.far_pair()
            own_half(2)
            rsy.give(1)
            own_half(3)
            gy.from_core()
            mm_rows(line_x.so)
            rsx.give(2)
            mm_rows(line_x.sp)
            rsx.give(0)
            mm_rows(line_x.sm)
            rsx.give(1)
            mm_rows(line_x.own)
        else:
            mm_rows(line_x.so)
            rsx.give(2)
            for i in (0, 1, 3):
                new_tile(i, 2)
            other_half(0)
            other_half(1)
            own_half(0)
            rsy.give(2)
            other_half(2)
            own_half(1)
            rsy.give(0)
            mm_rows(line_x.sp)
            rsx.give(0)
            other_half(3)
            own_half(2)
            rsy.give(1)
            mm_rows(line_x.sm)
            rsx.give(1)
            own_half(3)
            mm_rows(line_x.own)
        rsy.pair()
        if it == 0:

            @pl.loop(0, 8)
            def _(i):
                rows = pl.ds(pl.multiple_of(i * 128, 128), 128)
                weight[rows, :] = -COUPLING / (jnp.concatenate([e_row[rows, :]] * 16, axis=1) + e_col[...])

        rsx.pair()

        hx = [
            Gather(
                line_x, dr, k, agx_s.at[1 + 2 * it + k], agx_r.at[1 + 2 * it + k],
                relay_own=True, relay_pair=True,
            )
            for k in range(2)
        ]
        hy = [
            Gather(
                line_y, dc, k, agy_s.at[1 + 2 * it + k], agy_r.at[1 + 2 * it + k], half_c, other_c,
                relay_own=True, relay_pair=True,
            )
            for k in range(2)
        ]
        r0, r1 = part_of(dr, mine_r, 0), part_of(dr, mine_r, 1)
        c0, c1 = part_of(dc, mine_c, 0), part_of(dc, mine_c, 1)
        turn_c = turn(2 + 2 * it, c1, part_of(dr, line_y.own, 1), turn_from)
        turn_r_ = turn(3 + 2 * it, r0, part_of(dc, half_c + col, 0), turn_to)

        if it == 0:

            @pl.when(moves)
            def _():
                turn(1, own1, own_c, turn_from).wait_recv()

        c1[...] = (own_c[...].astype(F32) + rsy.total()).astype(BF16)

        @pl.when(moves)
        def _():
            turn_c.start()

        hy[1].start()
        r0[...] = (own0[...].astype(F32) + rsx.total()).astype(BF16)

        @pl.when(moves)
        def _():
            turn_r_.start()

        hx[0].start()

        @pl.when(stays)
        def _():
            r1[...] = c1[...]
            c0[...] = r0[...]

        hy[1].pair()
        hx[0].pair()

        @pl.when(moves)
        def _():
            turn(2 + 2 * it, r1, r1, turn_to).wait_recv()

        hx[1].start()

        @pl.when(moves)
        def _():
            turn(3 + 2 * it, c0, c0, turn_from).wait_recv()

        hy[0].start()
        hy[1].near()
        hx[0].near()
        hy[1].near_pair()
        hx[0].near_pair()
        hy[0].pair()
        hx[1].pair()
        hy[1].far()
        hx[0].far()
        hy[0].near()
        hx[1].near()
        hy[1].far_pair()
        hx[0].far_pair()
        hy[0].near_pair()
        hx[1].near_pair()
        if it == 0:
            hy[1].from_core()
            hy[0].from_core(0, 6)
            new_tiles(0)
            hy[0].far()
            hx[1].far()
            new_tiles(1)
            hy[0].far_pair()
            hx[1].far_pair()
            new_tiles(3)
            hy[0].from_core(6, 8)
            for j in (0, 1, 3, 2):
                new_tile(2, j)
        else:
            hy[0].far()
            hx[1].far()
            hy[0].far_pair()
            hx[1].far_pair()
            hy[1].from_core()
            hy[0].from_core()

        for i in range(4):
            core_copy(i).wait_send()
        for exchange in (rsx, rsy, *hx, *hy):
            exchange.sent()

        @pl.when(moves)
        def _():
            turn_c.wait_send()
            turn_r_.wait_send()

    gx.sent()
    gy.sent()

    @pl.when(moves)
    def _():
        turn_f0.wait_send()
        turn_f1.wait_send()


def dma(*shape):
    return pltpu.SemaphoreType.DMA(shape)


def shards(amplitudes, factors, energies):
    row_tile, col_tile = amplitudes.shape
    vmem = pl.BlockSpec(memory_space=pltpu.VMEM)

    def line_buffers():
        return [
            pltpu.VMEM((3, 2, SLOT, K), BF16),
            pltpu.VMEM((SLOT, K), BF16),
            pltpu.VMEM((2, 3, 2, SLOT, K), BF16),
            pltpu.VMEM((2, SLOT, K), BF16),
        ]

    energy = energies.reshape(128, 128)
    hbm = pl.BlockSpec(memory_space=pltpu.MemorySpace.HBM)
    dr, dc, e_row, e_col = pl.pallas_call(
        cycle,
        out_shape=(
            jax.ShapeDtypeStruct((row_tile, AUX), BF16),
            jax.ShapeDtypeStruct((col_tile, AUX), BF16),
            jax.ShapeDtypeStruct((row_tile, 128), F32),
            jax.ShapeDtypeStruct((1, col_tile), F32),
        ),
        in_specs=[hbm, hbm, hbm],
        out_specs=(vmem, vmem, vmem, vmem),
        scratch_shapes=[
            pltpu.VMEM((row_tile, col_tile), BF16),
            pltpu.VMEM((2, 256, col_tile), F32),
            pltpu.VMEM((SLOT, AUX), BF16),
            pltpu.VMEM((128, 128), F32),
            pltpu.VMEM((row_tile, K), BF16),
            pltpu.VMEM((col_tile, K), BF16),
            pltpu.VMEM((SLOT, K), BF16),
            pltpu.VMEM((row_tile, AUX), BF16),
            pltpu.VMEM((col_tile, AUX), BF16),
            pltpu.VMEM((row_tile, K), F32),
            pltpu.VMEM((row_tile, K), F32),
            pltpu.VMEM((4, 256, K), BF16),
            pltpu.VMEM((2, 4, 256, K), BF16),
            pltpu.VMEM((row_tile, col_tile), F32),
            *line_buffers(),
            *line_buffers(),
            dma(2), dma(2), dma(6), dma(6),
            dma(5, 20), dma(5, 20), dma(5, 20), dma(5, 20),
            dma(2, 7), dma(2, 7), dma(2, 7), dma(2, 7),
            dma(2, 4), dma(2, 4),
        ],
        compiler_params=pltpu.CompilerParams(
            collective_id=0, has_side_effects=True, vmem_limit_bytes=46 * 1024 * 1024
        ),
        name="cycle",
    )(*(pltpu.with_memory_space_constraint(v, pltpu.MemorySpace.HBM) for v in (amplitudes, factors, energy)))

    return pl.pallas_call(
        finish,
        out_shape=jax.ShapeDtypeStruct((row_tile, col_tile), F32),
        in_specs=[vmem, vmem, vmem, vmem],
        out_specs=pl.BlockSpec(memory_space=pl.ANY),
        scratch_shapes=[pltpu.VMEM((2, 4, 256, 512), F32), dma(2, 4)],
        compiler_params=pltpu.CompilerParams(vmem_limit_bytes=20 * 1024 * 1024),
        name="finish",
    )(dr, dc, e_row, e_col)


def solution(mesh):
    placed = (P("row", "col"), P(("row", "col"), None), P())
    return jax.shard_map(
        shards, mesh=mesh, in_specs=placed, out_specs=P("row", "col"), check_vma=False
    )
```

```python
import functools
import math

import jax
import jax.numpy as jnp
from jax import lax
from jax.experimental import pallas as pl
from jax.experimental.pallas import tpu as pltpu
from jax.sharding import PartitionSpec as P

ORDER = 16384
AUX = 768
COUPLING = ORDER / math.sqrt(AUX)
INV_ROOT = 1.0 / math.sqrt(ORDER)
MESH = pl.DeviceIdType.MESH
BF16, F32 = jnp.bfloat16, jnp.float32

SLOT = 128
HALF = SLOT // 2
K = AUX // 2
NT = (((1,), (1,)), ((), ()))
TN = (((0,), (0,)), ((), ()))


def part_of(ref, slot, k=None, offset=0, size=SLOT):
    rows = pl.ds(pl.multiple_of(slot * SLOT + offset, HALF), size)
    return ref.at[rows, :] if k is None else ref.at[rows, pl.ds(k * K, K)]


class Line:
    def __init__(self, device, slot, core=None):
        self.p, self.m, self.o, self.z = device(1, 0), device(3, 0), device(2, 0), device(0, 1)
        self.core = core
        self.own, self.own_z = slot(0, 0), slot(0, 1)
        self.sp, self.sp_z = slot(1, 0), slot(1, 1)
        self.sm, self.sm_z = slot(3, 0), slot(3, 1)
        self.so, self.so_z = slot(2, 0), slot(2, 1)


class Exchange:
    def __init__(self, send, recv):
        self.send, self.recv = send, recv
        self.started = []

    def copy(self, i, src, dst, target):
        return pltpu.make_async_remote_copy(
            src_ref=src, dst_ref=dst, send_sem=self.send.at[i], recv_sem=self.recv.at[i],
            device_id=target, device_id_type=MESH,
        )

    def go(self, i, src, dst, target):
        c = self.copy(i, src, dst, target)
        c.start()
        self.started.append(c)

    def got(self, i, dst, source):
        self.copy(i, dst, dst, source).wait_recv()

    def sent(self):
        for c in self.started:
            c.wait_send()
        self.started = []


class Gather(Exchange):
    def __init__(self, line, buf, k, send, recv, base=0, other=None, relay_own=False, relay_pair=False):
        super().__init__(send, recv)
        self.line, self.buf, self.k = line, buf, k
        self.base, self.other = base, other
        self.relay_own, self.relay_pair = relay_own, relay_pair

    def view(self, slot, offset=0, size=SLOT):
        return part_of(self.buf, self.base + slot, self.k, offset, size)

    def push(self, i, slot, target, offset=0, size=SLOT, src=None):
        dst = self.view(slot, offset, size)
        self.go(i, dst if src is None else src, dst, target)

    def arrived(self, i, slot, source, offset=0, size=SLOT):
        self.got(i, self.view(slot, offset, size), source)

    def to_core(self, i, slot):
        if self.other is not None:
            self.push(9 + i, slot, self.line.core)

    def start(self, src=None):
        ln = self.line
        for h in range(2):
            half = None if src is None else src.at[pl.ds(h * HALF, HALF), :]
            self.push(17 * h + 2 * (1 - h), ln.own, ln.z, h * HALF, HALF, src=half)
        if not self.relay_own:
            self.push(5, ln.own, ln.o, src=src)
        self.push(0, ln.own, ln.p, src=src)
        self.push(1, ln.own, ln.m, src=src)
        self.to_core(0, ln.own)

    def pair(self):
        ln = self.line
        for h, (i, to_p, to_m) in enumerate(((2, 3, 4), (17, 18, 19))):
            self.arrived(i, ln.own_z, ln.z, h * HALF, HALF)
            if not self.relay_pair:
                self.push(7 + h, ln.own_z, ln.o, h * HALF, HALF)
            self.push(to_p, ln.own_z, ln.p, h * HALF, HALF)
            self.push(to_m, ln.own_z, ln.m, h * HALF, HALF)
        self.to_core(1, ln.own_z)

    def near(self):
        ln = self.line
        self.arrived(0, ln.sm, ln.m)
        if self.relay_own:
            self.push(5, ln.sm, ln.p, 0, HALF)
        self.to_core(2, ln.sm)
        self.arrived(1, ln.sp, ln.p)
        if self.relay_own:
            self.push(6, ln.sp, ln.m, HALF, HALF)
        self.to_core(3, ln.sp)

    def near_pair(self):
        ln = self.line
        self.arrived(3, ln.sm_z, ln.m, 0, HALF)
        if self.relay_pair:
            self.push(7, ln.sm_z, ln.p, 0, HALF)
        self.arrived(19, ln.sp_z, ln.p, HALF, HALF)
        if self.relay_pair:
            self.push(8, ln.sp_z, ln.m, HALF, HALF)
        self.arrived(18, ln.sm_z, ln.m, HALF, HALF)
        self.to_core(4, ln.sm_z)
        self.arrived(4, ln.sp_z, ln.p, 0, HALF)
        self.to_core(5, ln.sp_z)

    def far(self):
        ln = self.line
        if self.relay_own:
            self.arrived(5, ln.so, ln.m, 0, HALF)
            self.arrived(6, ln.so, ln.p, HALF, HALF)
        else:
            self.arrived(5, ln.so, ln.o)
        self.to_core(6, ln.so)

    def far_pair(self):
        ln = self.line
        if self.relay_pair:
            self.arrived(7, ln.so_z, ln.m, 0, HALF)
            self.arrived(8, ln.so_z, ln.p, HALF, HALF)
        else:
            self.arrived(7, ln.so_z, ln.o, 0, HALF)
            self.arrived(8, ln.so_z, ln.o, HALF, HALF)
        self.to_core(7, ln.so_z)

    def from_core(self, first=0, last=8):
        ln = self.line
        order = (ln.own, ln.own_z, ln.sm, ln.sp, ln.sm_z, ln.sp_z, ln.so, ln.so_z)
        for i in range(first, last):
            self.got(9 + i, part_of(self.buf, self.other + order[i], self.k), ln.core)


class Reduce(Exchange):
    def __init__(self, line, part, out, outz, into, inz, send, recv):
        super().__init__(send, recv)
        self.line, self.part = line, part
        self.out, self.outz, self.into, self.inz = out, outz, into, inz

    def give(self, d):
        ln = self.line
        slots, target = (
            ((ln.sp_z, ln.sp), ln.p), ((ln.sm_z, ln.sm), ln.m), ((ln.so_z, ln.so), ln.o),
        )[d]
        for h in range(2):
            self.out[d, h] = part_of(self.part, slots[h])[...].astype(BF16)
            self.go(2 * d + h, self.out.at[d, h], self.into.at[d, h], target)

    def collect(self, h):
        ln = self.line
        for d, source in ((0, ln.m), (1, ln.p), (2, ln.o)):
            self.got(2 * d + h, self.into.at[d, h], source)
        total = part_of(self.part, ln.own if h else ln.own_z)[...]
        for d in range(3):
            total = total + self.into[d, h].astype(F32)
        return total

    def pair(self):
        self.outz[...] = self.collect(0).astype(BF16)
        self.go(6, self.outz, self.inz, self.line.z)

    def total(self):
        total = self.collect(1)
        self.got(6, self.inz, self.line.z)
        return total + self.inz[...].astype(F32)


def spread_energies(energy, e_row, e_col):
    row, col = lax.axis_index("row"), lax.axis_index("col")
    for j in range(8):
        v = energy[pl.ds(row * 8 + j, 1), :]
        e_row[j * 128 : (j + 1) * 128, :] = jnp.broadcast_to(v, (128, 128)).T
    for j in range(16):
        e_col[:, j * 128 : (j + 1) * 128] = energy[pl.ds(col * 16 + j, 1), :]


def tile(dr, dc, e_row, e_col):
    residual = lax.dot_general(dr, dc, NT, preferred_element_type=F32)
    den = jnp.concatenate([e_row] * (residual.shape[1] // 128), axis=1) + e_col
    return -COUPLING * residual / den


def finish(dr, dc, e_row, e_col, out, stage, sem):
    def put(i, j):
        part = out.at[pl.ds(i * 256, 256), pl.ds(j * 512, 512)]
        return pltpu.make_async_copy(stage.at[i % 2, j], part, sem.at[i % 2, j])

    for i in range(4):
        rows = slice(i * 256, (i + 1) * 256)
        for j in range(4):
            cols = slice(j * 512, (j + 1) * 512)
            if i >= 2:
                put(i - 2, j).wait()
            stage[i % 2, j] = tile(dr[rows, :], dc[cols, :], e_row[rows, :], e_col[:, cols])
            put(i, j).start()
    for i in (2, 3):
        for j in range(4):
            put(i, j).wait()


def cycle(
    amp, own_hbm, energy_hbm, dr1, dc1, e_row, e_col,
    a, stage, own, energy, fr, fc, own_c, dr0, dc0, part_r, part_c, core_out, core_in, weight,
    x_out, x_outz, x_in, x_inz, y_out, y_outz, y_in, y_inz,
    amp_sem, in_sem, turn_s, turn_r, agx_s, agx_r, agy_s, agy_r, rsx_s, rsx_r, rsy_s, rsy_r, co_s, co_r,
):
    row, col = lax.axis_index("row"), lax.axis_index("col")
    core, chip_row = lax.rem(row, 2), row // 2
    hi, y = chip_row // 4, lax.rem(chip_row, 4)
    x, lo = col // 2, lax.rem(col, 2)

    def at(r, c):
        return {"row": r, "col": c}

    def x_slot(step, flip):
        return lax.rem(x + step, 4) * 2 + (1 - lo if flip else lo)

    first_y = lax.rem(x, 2) * 2 + lo
    parity = x // 2 + lo

    def y_slot(step, flip):
        z = 1 - hi if flip else hi
        return lax.rem(x + y + step + 4 - first_y, 4) * 2 + lax.rem(z + parity, 2)

    def dev_x(step, flip):
        return at(row, x_slot(step, flip))

    def dev_y(step, flip):
        z = 1 - hi if flip else hi
        return at((z * 4 + lax.rem(y + step, 4)) * 2 + core, col)

    partner = at(chip_row * 2 + 1 - core, col)
    line_x = Line(dev_x, x_slot)
    line_y = Line(dev_y, y_slot, partner)

    x_to = chip_row // 2
    y_to = lax.rem(y + x + 4 - x_to, 4)
    hi_to = lax.rem(hi + lo + y, 2)
    to_row, to_col = (hi_to * 4 + y_to) * 2 + core, x_to * 2 + lax.rem(y, 2)
    turn_to = at(to_row, to_col)
    turn_from = at(col * 2 + core, line_y.own)
    moves = (to_row - row) * (to_row - row) + (to_col - col) * (to_col - col) != 0
    stays = jnp.logical_not(moves)

    half_c, other_c = core * 8, (1 - core) * 8
    mine_r, mine_c = line_x.own, half_c + line_y.own

    def turn(i, src, dst, device):
        return pltpu.make_async_remote_copy(
            src_ref=src, dst_ref=dst, send_sem=turn_s.at[i], recv_sem=turn_r.at[i],
            device_id=device, device_id_type=MESH,
        )

    def amp_copy(i):
        return pltpu.make_async_copy(amp.at[pl.ds(i * 256, 256), :], stage.at[i % 2], amp_sem.at[i % 2])

    own_copy = pltpu.make_async_copy(own_hbm, own, in_sem.at[0])
    energy_copy = pltpu.make_async_copy(energy_hbm, energy, in_sem.at[1])
    own_copy.start()
    energy_copy.start()
    amp_copy(0).start()
    amp_copy(1).start()

    barrier = pltpu.get_barrier_semaphore()

    def greet(device):
        pl.semaphore_signal(barrier, inc=1, device_id=device, device_id_type=MESH)

    for ln in (line_x, line_y):
        for device in (ln.p, ln.m, ln.o, ln.z):
            greet(device)
    greet(partner)

    @pl.when(moves)
    def _():
        greet(turn_to)
        greet(turn_from)

    def take_amp(i):
        amp_copy(i).wait()
        a[i * 256 : (i + 1) * 256, :] = stage[i % 2].astype(BF16)
        if i + 2 < 4:
            amp_copy(i + 2).start()

    own_copy.wait()
    take_amp(0)

    @pl.when(moves)
    def _():
        pl.semaphore_wait(barrier, 11)

    @pl.when(stays)
    def _():
        pl.semaphore_wait(barrier, 9)

    gx = Gather(line_x, fr, None, agx_s.at[0], agx_r.at[0], relay_own=True, relay_pair=True)
    gy = Gather(line_y, fc, None, agy_s.at[0], agy_r.at[0], half_c, other_c, relay_own=True)
    own0, own1 = own.at[:, pl.ds(0, K)], own.at[:, pl.ds(K, K)]
    turn_f0 = turn(0, own0, part_of(fc, half_c + col), turn_to)
    turn_f1 = turn(1, own1, own_c, turn_to)

    @pl.when(moves)
    def _():
        turn_f0.start()

    gx.start(src=own1)
    part_of(fr, mine_r)[...] = own1[...]

    @pl.when(stays)
    def _():
        part_of(fc, mine_c)[...] = own0[...]
        own_c[...] = own1[...]

    take_amp(1)
    take_amp(2)
    gx.pair()
    take_amp(3)
    energy_copy.wait()
    spread_energies(energy, e_row, e_col)

    @pl.when(moves)
    def _():
        turn(0, own0, part_of(fc, mine_c), turn_from).wait_recv()

    gy.start()
    gx.near()
    gy.pair()
    gx.near_pair()
    gx.far()
    gy.near()
    gx.far_pair()

    @pl.when(moves)
    def _():
        turn_f1.start()


    def mm_rows(s):
        at_rows = pl.ds(pl.multiple_of((s // 2) * 256, 256), 256)
        part_r[at_rows, :] = jnp.dot(a[at_rows, :], fc[...], preferred_element_type=F32) * INV_ROOT

    def mm_cols(half, s, s_z):
        lhs = [a[:, pl.ds(pl.multiple_of((half + i) * SLOT, SLOT), SLOT)] for i in (s, s_z)]
        lhs = jnp.concatenate(lhs, axis=1)
        return lax.dot_general(lhs, fr[...], TN, preferred_element_type=F32) * INV_ROOT

    def new_tile(i, j):
        rows = pl.ds(pl.multiple_of(lax.rem(x + i, 4) * 256, 256), 256)
        first = lax.rem(x + y + j + 4 - first_y, 4) * 256
        cols = [pl.ds(pl.multiple_of(h * 1024 + first, 256), 256) for h in range(2)]
        residual = lax.dot_general(
            dr0[rows, :], jnp.concatenate([dc0[c, :] for c in cols], axis=0), NT, preferred_element_type=F32
        )
        for h in range(2):
            a[rows, cols[h]] = (residual[:, h * 256 : (h + 1) * 256] * weight[rows, cols[h]]).astype(BF16)

    def new_tiles(i):
        for j in (0, 1, 3):
            new_tile(i, j)

    pairs_y = (
        (line_y.so, line_y.so_z), (line_y.sp, line_y.sp_z), (line_y.sm, line_y.sm_z), (line_y.own, line_y.own_z),
    )

    for it in range(2):
        dr, dc = (dr0, dc0) if it == 0 else (dr1, dc1)
        rsx = Reduce(line_x, part_r, x_out, x_outz, x_in.at[it], x_inz.at[it], rsx_s.at[it], rsx_r.at[it])
        rsy = Reduce(line_y, part_c, y_out, y_outz, y_in.at[it], y_inz.at[it], rsy_s.at[it], rsy_r.at[it])

        def core_copy(i):
            return pltpu.make_async_remote_copy(
                src_ref=core_out.at[i], dst_ref=core_in.at[it, i],
                send_sem=co_s.at[it, i], recv_sem=co_r.at[it, i],
                device_id=partner, device_id_type=MESH,
            )

        def other_half(i):
            core_out[i] = mm_cols(other_c, *pairs_y[i]).astype(BF16)
            core_copy(i).start()

        def own_half(i):
            value = mm_cols(half_c, *pairs_y[i])
            core_copy(i).wait_recv()
            value = value + core_in[it, i].astype(F32)
            part_of(part_c, pairs_y[i][0])[...] = value[:SLOT]
            part_of(part_c, pairs_y[i][1])[...] = value[SLOT:]

        if it == 0:
            other_half(0)
            other_half(1)
            gy.near_pair()
            other_half(2)
            other_half(3)
            own_half(0)
            rsy.give(2)
            own_half(1)
            rsy.give(0)
            gy.far()
            gy.far_pair()
            own_half(2)
            rsy.give(1)
            own_half(3)
            gy.from_core()
            mm_rows(line_x.so)
            rsx.give(2)
            mm_rows(line_x.sp)
            rsx.give(0)
            mm_rows(line_x.sm)
            rsx.give(1)
            mm_rows(line_x.own)
        else:
            mm_rows(line_x.so)
            rsx.give(2)
            for i in (0, 1, 3):
                new_tile(i, 2)
            other_half(0)
            other_half(1)
            own_half(0)
            rsy.give(2)
            other_half(2)
            own_half(1)
            rsy.give(0)
            mm_rows(line_x.sp)
            rsx.give(0)
            other_half(3)
            own_half(2)
            rsy.give(1)
            mm_rows(line_x.sm)
            rsx.give(1)
            own_half(3)
            mm_rows(line_x.own)
        rsy.pair()
        if it == 0:

            @pl.loop(0, 8)
            def _(i):
                rows = pl.ds(pl.multiple_of(i * 128, 128), 128)
                weight[rows, :] = -COUPLING / (jnp.concatenate([e_row[rows, :]] * 16, axis=1) + e_col[...])

        rsx.pair()

        hx = [
            Gather(
                line_x, dr, k, agx_s.at[1 + 2 * it + k], agx_r.at[1 + 2 * it + k],
                relay_own=True, relay_pair=True,
            )
            for k in range(2)
        ]
        hy = [
            Gather(
                line_y, dc, k, agy_s.at[1 + 2 * it + k], agy_r.at[1 + 2 * it + k], half_c, other_c,
                relay_own=True, relay_pair=True,
            )
            for k in range(2)
        ]
        r0, r1 = part_of(dr, mine_r, 0), part_of(dr, mine_r, 1)
        c0, c1 = part_of(dc, mine_c, 0), part_of(dc, mine_c, 1)
        turn_c = turn(2 + 2 * it, c1, part_of(dr, line_y.own, 1), turn_from)
        turn_r_ = turn(3 + 2 * it, r0, part_of(dc, half_c + col, 0), turn_to)

        if it == 0:

            @pl.when(moves)
            def _():
                turn(1, own1, own_c, turn_from).wait_recv()

        c1[...] = (own_c[...].astype(F32) + rsy.total()).astype(BF16)

        @pl.when(moves)
        def _():
            turn_c.start()

        hy[1].start()
        r0[...] = (own0[...].astype(F32) + rsx.total()).astype(BF16)

        @pl.when(moves)
        def _():
            turn_r_.start()

        hx[0].start()

        @pl.when(stays)
        def _():
            r1[...] = c1[...]
            c0[...] = r0[...]

        hy[1].pair()
        hx[0].pair()

        @pl.when(moves)
        def _():
            turn(2 + 2 * it, r1, r1, turn_to).wait_recv()

        hx[1].start()

        @pl.when(moves)
        def _():
            turn(3 + 2 * it, c0, c0, turn_from).wait_recv()

        hy[0].start()
        hy[1].near()
        hx[0].near()
        hy[0].pair()
        hx[1].pair()
        hy[1].near_pair()
        hx[0].near_pair()
        hy[1].far()
        hx[0].far()
        hy[0].near()
        hx[1].near()
        hy[1].far_pair()
        hx[0].far_pair()
        hy[0].near_pair()
        hx[1].near_pair()
        if it == 0:
            hy[1].from_core()
            hy[0].from_core(0, 6)
            new_tiles(0)
            hy[0].far()
            hx[1].far()
            new_tiles(1)
            hy[0].far_pair()
            hx[1].far_pair()
            new_tiles(3)
            hy[0].from_core(6, 8)
            for j in (0, 1, 3, 2):
                new_tile(2, j)
        else:
            hy[0].far()
            hx[1].far()
            hy[0].far_pair()
            hx[1].far_pair()
            hy[1].from_core()
            hy[0].from_core()

        for i in range(4):
            core_copy(i).wait_send()
        for exchange in (rsx, rsy, *hx, *hy):
            exchange.sent()

        @pl.when(moves)
        def _():
            turn_c.wait_send()
            turn_r_.wait_send()

    gx.sent()
    gy.sent()

    @pl.when(moves)
    def _():
        turn_f0.wait_send()
        turn_f1.wait_send()


def dma(*shape):
    return pltpu.SemaphoreType.DMA(shape)


def shards(amplitudes, factors, energies):
    row_tile, col_tile = amplitudes.shape
    vmem = pl.BlockSpec(memory_space=pltpu.VMEM)

    def line_buffers():
        return [
            pltpu.VMEM((3, 2, SLOT, K), BF16),
            pltpu.VMEM((SLOT, K), BF16),
            pltpu.VMEM((2, 3, 2, SLOT, K), BF16),
            pltpu.VMEM((2, SLOT, K), BF16),
        ]

    energy = energies.reshape(128, 128)
    hbm = pl.BlockSpec(memory_space=pltpu.MemorySpace.HBM)
    dr, dc, e_row, e_col = pl.pallas_call(
        cycle,
        out_shape=(
            jax.ShapeDtypeStruct((row_tile, AUX), BF16),
            jax.ShapeDtypeStruct((col_tile, AUX), BF16),
            jax.ShapeDtypeStruct((row_tile, 128), F32),
            jax.ShapeDtypeStruct((1, col_tile), F32),
        ),
        in_specs=[hbm, hbm, hbm],
        out_specs=(vmem, vmem, vmem, vmem),
        scratch_shapes=[
            pltpu.VMEM((row_tile, col_tile), BF16),
            pltpu.VMEM((2, 256, col_tile), F32),
            pltpu.VMEM((SLOT, AUX), BF16),
            pltpu.VMEM((128, 128), F32),
            pltpu.VMEM((row_tile, K), BF16),
            pltpu.VMEM((col_tile, K), BF16),
            pltpu.VMEM((SLOT, K), BF16),
            pltpu.VMEM((row_tile, AUX), BF16),
            pltpu.VMEM((col_tile, AUX), BF16),
            pltpu.VMEM((row_tile, K), F32),
            pltpu.VMEM((row_tile, K), F32),
            pltpu.VMEM((4, 256, K), BF16),
            pltpu.VMEM((2, 4, 256, K), BF16),
            pltpu.VMEM((row_tile, col_tile), F32),
            *line_buffers(),
            *line_buffers(),
            dma(2), dma(2), dma(6), dma(6),
            dma(5, 20), dma(5, 20), dma(5, 20), dma(5, 20),
            dma(2, 7), dma(2, 7), dma(2, 7), dma(2, 7),
            dma(2, 4), dma(2, 4),
        ],
        compiler_params=pltpu.CompilerParams(
            collective_id=0, has_side_effects=True, vmem_limit_bytes=46 * 1024 * 1024
        ),
        name="cycle",
    )(*(pltpu.with_memory_space_constraint(v, pltpu.MemorySpace.HBM) for v in (amplitudes, factors, energy)))

    return pl.pallas_call(
        finish,
        out_shape=jax.ShapeDtypeStruct((row_tile, col_tile), F32),
        in_specs=[vmem, vmem, vmem, vmem],
        out_specs=pl.BlockSpec(memory_space=pl.ANY),
        scratch_shapes=[pltpu.VMEM((2, 4, 256, 512), F32), dma(2, 4)],
        compiler_params=pltpu.CompilerParams(vmem_limit_bytes=20 * 1024 * 1024),
        name="finish",
    )(dr, dc, e_row, e_col)


def solution(mesh):
    placed = (P("row", "col"), P(("row", "col"), None), P())
    return jax.shard_map(
        shards, mesh=mesh, in_specs=placed, out_specs=P("row", "col"), check_vma=False
    )
```
